512 devices in a mesh: gx: 16 (over z), gy: 32 (over y, x, core).
Axes of the slice: x: 4, y: 4, z: 16, core: 2. Of those that a mesh axis runs over, the one named last changes fastest.
Arguments:
- initial_temp: float32 [1, 8192, 8192], P(None, 'gy', 'gx'), may hold values from -8 to 8
- kx_low: float32 [1, 8192, 8192], P(None, 'gy', 'gx'), may hold values from 6e-06 to 2000000
- ky_low: float32 [1, 8192, 8192], P(None, 'gy', 'gx'), may hold values from 6e-06 to 2000000
Outputs:
- new_temp: float32 [1, 8192, 8192], P(None, 'gy', 'gx')
The draws below stay inside these ranges and needn't reach their ends.
All inputs are finite; a program needn't handle non-finite values.
Results may differ from the reference program's by a relative error of at most 0.00002.
Values sent between devices are 32-bit elements; how exact they have to be, the bound alone decides.
A program may use at most 64 MiB of HBM per device.

```python
import math
import jax
import jax.numpy as jnp
from jax import lax

LEV = 1
NX = 8192
NY = 8192


def draw_initial_temp(key, part):
    base_key = jax.random.fold_in(key, 5)
    subkeys = jax.random.split(base_key, 3)
    full_shape = (LEV, NY, NX)
    rough_part = jnp.clip(jax.random.normal(subkeys[0], full_shape, jnp.float32), -4.0, 4.0)
    amplitudes = jax.random.uniform(subkeys[1], (LEV, 6), jnp.float32, -0.6, 0.6)
    phases = jax.random.uniform(subkeys[2], (LEV, 6), jnp.float32, 0.0, 2.0 * math.pi)
    along_x = jnp.arange(NX, dtype=jnp.float32) / NX
    along_y = jnp.arange(NY, dtype=jnp.float32) / NY
    wave_x = jnp.zeros((LEV, NX), jnp.float32)
    wave_y = jnp.zeros((LEV, NY), jnp.float32)
    for mode_index in range(3):
        wave_x = wave_x + amplitudes[:, mode_index:mode_index + 1] * jnp.cos(2.0 * math.pi * (mode_index + 1) * along_x[None, :] + phases[:, mode_index:mode_index + 1])
        wave_y = wave_y + amplitudes[:, mode_index + 3:mode_index + 4] * jnp.cos(2.0 * math.pi * (mode_index + 1) * along_y[None, :] + phases[:, mode_index + 3:mode_index + 4])
    combined = rough_part + wave_y[:, :, None] + wave_x[:, None, :]
    return jnp.clip(combined, -8.0, 8.0)


def face_conductivity(base_key, along_lines_x):
    subkeys = jax.random.split(base_key, 6)
    full_shape = (LEV, NY, NX)
    if along_lines_x:
        line_shape = (LEV, NY, 1)
        line_dim = 2
        line_length = NX
    else:
        line_shape = (LEV, 1, NX)
        line_dim = 1
        line_length = NY
    exponent = jax.random.uniform(subkeys[0], line_shape, jnp.float32, -1.0, 6.0)
    spread = jnp.exp(jax.random.uniform(subkeys[1], full_shape, jnp.float32, math.log(0.5), math.log(2.0)))
    positions = lax.broadcasted_iota(jnp.int32, full_shape, line_dim)
    barrier = jnp.ones(full_shape, jnp.float32)
    for barrier_index in range(3):
        barrier_spot = jax.random.randint(subkeys[2 + barrier_index], line_shape, 0, line_length)
        barrier = barrier * jnp.where(positions == barrier_spot, 0.05, 1.0)
    return jnp.power(10.0, exponent) * spread * barrier


def draw_kx_low(key, part):
    return face_conductivity(jax.random.fold_in(key, 11), True)


def draw_ky_low(key, part):
    return face_conductivity(jax.random.fold_in(key, 23), False)


def setup_inputs(seed: int = 0) -> dict:
    streams_of = jax.random.split(jax.random.key(seed), 4)
    initial_temp = draw_initial_temp(jax.random.fold_in(streams_of[3], 71), 0)
    kx_low = draw_kx_low(jax.random.fold_in(streams_of[3], 71), 0)
    ky_low = draw_ky_low(jax.random.fold_in(streams_of[3], 71), 0)
    return {"initial_temp": initial_temp, "kx_low": kx_low, "ky_low": ky_low}


def periodic_solve(low_face, source):
    upper_face = jnp.roll(low_face, -1, axis=-1)
    lower_band = -low_face
    upper_band = -upper_face
    excess = jnp.ones_like(source)
    length = source.shape[-1]
    stride = 1
    while stride < length:
        lower_below = jnp.roll(lower_band, stride, axis=-1)
        upper_below = jnp.roll(upper_band, stride, axis=-1)
        excess_below = jnp.roll(excess, stride, axis=-1)
        source_below = jnp.roll(source, stride, axis=-1)
        lower_above = jnp.roll(lower_band, -stride, axis=-1)
        upper_above = jnp.roll(upper_band, -stride, axis=-1)
        excess_above = jnp.roll(excess, -stride, axis=-1)
        source_above = jnp.roll(source, -stride, axis=-1)
        alpha_coef = -lower_band / (excess_below - lower_below - upper_below)
        gamma_coef = -upper_band / (excess_above - lower_above - upper_above)
        excess = excess + alpha_coef * excess_below + gamma_coef * excess_above
        source = source + alpha_coef * source_below + gamma_coef * source_above
        lower_band = alpha_coef * lower_below
        upper_band = gamma_coef * upper_above
        stride = stride * 2
    return source / excess


def reference(initial_temp, kx_low, ky_low):
    half_step = periodic_solve(kx_low, initial_temp)
    turned = periodic_solve(jnp.swapaxes(ky_low, 1, 2), jnp.swapaxes(half_step, 1, 2))
    return jnp.swapaxes(turned, 1, 2)
```

```python
import functools

import jax
import jax.numpy as jnp
from jax import lax
from jax.experimental import pallas as pl
from jax.experimental.pallas import tpu as pltpu
from jax.sharding import PartitionSpec as P

MESH = pl.DeviceIdType.MESH
SUB = 8
LANES = 128
WAYS = 4
REACH = 4
SHORT = 1e30


def recip(value):
    return pltpu.reciprocal(value, full_range=False)


def join_matrix(low, high):
    excess = low[1] + high[2]
    inverse = recip(excess + (low[0] + high[0]))
    to_low = low[0] * inverse
    to_high = high[0] * inverse
    joined = (to_low * high[0], high[1] + to_high * excess, low[2] + to_low * excess)
    return joined, (inverse, to_low, to_high)


def join_source(low, high, coefs):
    inverse, to_low, to_high = coefs
    source = low[0] + high[1]
    return (high[0] + to_high * source, low[1] + to_low * source), source * inverse


def next_rows(value, steps):
    return pltpu.roll(value, SUB - steps, 1)


def tree_matrix(blocks, coef_ref, lanes):
    def keep(slot, coefs):
        for place, coef in enumerate(coefs):
            coef_ref[3 * slot + place, lanes] = coef

    first, coefs = join_matrix(blocks[0], blocks[1])
    keep(0, coefs)
    second, coefs = join_matrix(blocks[2], blocks[3])
    keep(1, coefs)
    joined, coefs = join_matrix(first, second)
    keep(2, coefs)
    for level in range(3):
        other = tuple(next_rows(member, 1 << level) for member in joined)
        joined, coefs = join_matrix(joined, other)
        keep(3 + level, coefs)
    return joined


def tree_source(blocks, coef_ref, mid_ref, lanes):
    def coefs(slot):
        return tuple(coef_ref[3 * slot + place, lanes] for place in range(3))

    first, mid = join_source(blocks[0], blocks[1], coefs(0))
    mid_ref[0, lanes] = mid
    second, mid = join_source(blocks[2], blocks[3], coefs(1))
    mid_ref[1, lanes] = mid
    joined, mid = join_source(first, second, coefs(2))
    mid_ref[2, lanes] = mid
    for level in range(3):
        other = tuple(next_rows(member, 1 << level) for member in joined)
        joined, mid = join_source(joined, other, coefs(3 + level))
        mid_ref[3 + level, lanes] = mid
    return joined


def spread(value, level, row):
    for bit in range(level + 1):
        value = jnp.where((row & (1 << bit)) != 0, pltpu.roll(value, 1 << bit, 1), value)
    return value


def spread_coefs(coef_ref, lanes, row):
    for level in range(3):
        for place in (1, 2):
            slot = 3 * (3 + level) + place
            coef_ref[slot, lanes] = spread(coef_ref[slot, lanes], level, row)


def spread_mids(mid_ref, lanes, row):
    for level in range(3):
        mid_ref[3 + level, lanes] = spread(mid_ref[3 + level, lanes], level, row)


def tree_down(left, right, coef_ref, mid_ref, lanes, row):
    def middle(slot, low, high):
        return (
            mid_ref[slot, lanes]
            + coef_ref[3 * slot + 1, lanes] * low
            + coef_ref[3 * slot + 2, lanes] * high
        )

    for level in (2, 1, 0):
        mid = middle(3 + level, left, right)
        lower = (row & (1 << level)) == 0
        left, right = jnp.where(lower, left, mid), jnp.where(lower, mid, right)
    center = middle(2, left, right)
    lower_mid = middle(0, left, center)
    upper_mid = middle(1, center, right)
    return (left, lower_mid, center, upper_mid, right)


def solve_pair(own_matrix, own_source, rest_matrix, rest_source):
    link = own_matrix[0] + rest_matrix[0]
    own_excess = own_matrix[1] + rest_matrix[2]
    prev_excess = own_matrix[2] + rest_matrix[1]
    own_total = own_source[0] + rest_source[1]
    prev_total = own_source[1] + rest_source[0]
    inverse = recip(own_excess * prev_excess + link * (own_excess + prev_excess))
    both = link * (own_total + prev_total)
    own_value = (own_total * prev_excess + both) * inverse
    prev_value = (prev_total * own_excess + both) * inverse
    return own_value, prev_value


def kernel(
    count_x,
    count_y,
    temp_hbm,
    kx_hbm,
    ky_hbm,
    out_hbm,
    temp_ref,
    kx_ref,
    ky_ref,
    temp_turned,
    kx_turned,
    half_ref,
    x_link,
    x_next,
    x_mid,
    y_link,
    y_next,
    y_inverse,
    y_mid,
    x_coefs,
    x_mids,
    y_coefs,
    y_mids,
    ring_coefs,
    ring_mids,
    x_send,
    x_pair_send,
    x_recv,
    x_pair_recv,
    y_matrix_send,
    y_matrix_recv,
    y_source_send,
    y_source_recv,
    in_sems,
    out_sems,
    x_send_sems,
    x_recv_sems,
    pair_send_sems,
    pair_recv_sems,
    matrix_send_sems,
    matrix_recv_sems,
    source_send_sems,
    source_recv_sems,
):
    rows, columns = temp_ref.shape
    blocks_x = rows // LANES
    blocks_y = columns // LANES
    my_x = lax.axis_index("gx")
    my_y = lax.axis_index("gy")
    loads = [
        pltpu.make_async_copy(kx_hbm, kx_ref, in_sems.at[0]),
        pltpu.make_async_copy(temp_hbm, temp_ref, in_sems.at[1]),
    ] + [
        pltpu.make_async_copy(
            ky_hbm.at[:, pl.ds(LANES * block, LANES)], ky_ref.at[block], in_sems.at[2 + block]
        )
        for block in range(blocks_y)
    ]
    for load in loads:
        load.start()

    def peer_x(offset):
        return {"gx": lax.rem(my_x + (offset + count_x), count_x)}

    def peer_y(offset):
        return {"gy": lax.rem(my_y + offset, count_y)}

    offsets = [sign * step for step in range(REACH, 0, -1) for sign in (1, -1)]
    barrier = pltpu.get_barrier_semaphore()
    for offset in offsets:
        pl.semaphore_signal(barrier, inc=1, device_id=peer_x(offset), device_id_type=MESH)
    for offset in range(1, count_y):
        pl.semaphore_signal(barrier, inc=1, device_id=peer_y(offset), device_id_type=MESH)

    def slot_of(offset):
        return offset + REACH - (1 if offset > 0 else 0)

    shape_x = (blocks_x, SUB, LANES)
    row_x = lax.broadcasted_iota(jnp.int32, shape_x, 1)
    every = slice(0, blocks_x)
    length_x = columns // (WAYS * SUB)
    length_y = rows // (WAYS * SUB)

    def rows_of(way, step, length):
        return pl.ds(way * length + step, SUB, stride=WAYS * length)

    def turn_in(source, target):
        for block in range(blocks_x):
            for left in range(0, columns, LANES):
                target[block, left : left + LANES, :] = source[
                    LANES * block : LANES * (block + 1), left : left + LANES
                ].T

    loads[0].wait()
    turn_in(kx_ref, kx_turned)
    loads[1].wait()
    turn_in(temp_ref, temp_turned)

    excess = [jnp.ones(shape_x, jnp.float32)] * WAYS
    link = [kx_turned[:, rows_of(way, 0, length_x), :] for way in range(WAYS)]
    source = [temp_turned[:, rows_of(way, 0, length_x), :] for way in range(WAYS)]
    left_excess = [jnp.zeros(shape_x, jnp.float32)] * WAYS
    left_source = [jnp.zeros(shape_x, jnp.float32)] * WAYS
    for step in range(length_x - 1):
        for way in range(WAYS):
            face = kx_turned[:, rows_of(way, step + 1, length_x), :]
            inverse = recip(excess[way] + link[way] + face)
            to_next = face * inverse
            to_left = link[way] * inverse
            x_next[step, way] = to_next
            x_link[step, way] = to_left
            x_mid[step, way] = source[way] * inverse
            left_excess[way] = left_excess[way] + to_left * excess[way]
            left_source[way] = left_source[way] + to_left * source[way]
            link[way] = to_left * face
            excess[way] = 1.0 + to_next * excess[way]
            source[way] = (
                temp_turned[:, rows_of(way, step + 1, length_x), :] + to_next * source[way]
            )
    matrix = [(link[way], excess[way], left_excess[way]) for way in range(WAYS)]
    own_matrix = tree_matrix(matrix, x_coefs, every)
    own_source = tree_source(
        [(source[way], left_source[way]) for way in range(WAYS)], x_coefs, x_mids, every
    )
    for place, member in enumerate(own_matrix + own_source):
        x_send[:, place : place + 1, :] = member[:, 0:1, :]

    pl.semaphore_wait(barrier, len(offsets) + count_y - 1)

    x_copies = {}
    for offset in offsets:
        x_copies[offset] = pltpu.make_async_remote_copy(
            src_ref=x_send,
            dst_ref=x_recv.at[slot_of(-offset)],
            send_sem=x_send_sems.at[slot_of(offset)],
            recv_sem=x_recv_sems.at[slot_of(-offset)],
            device_id=peer_x(offset),
            device_id_type=MESH,
        )
        x_copies[offset].start()

    for load in loads[2:]:
        load.wait()
    width = 2
    shape_y = (width, SUB, LANES)
    groups = [slice(start, start + width) for start in range(0, blocks_y, width)]
    row_y = lax.broadcasted_iota(jnp.int32, shape_y, 1)
    for lanes in groups:
        excess = [jnp.ones(shape_y, jnp.float32)] * WAYS
        link = [ky_ref[lanes, rows_of(way, 0, length_y), :] for way in range(WAYS)]
        left_excess = [jnp.zeros(shape_y, jnp.float32)] * WAYS
        for step in range(length_y - 1):
            for way in range(WAYS):
                face = ky_ref[lanes, rows_of(way, step + 1, length_y), :]
                inverse = recip(excess[way] + link[way] + face)
                to_next = face * inverse
                to_left = link[way] * inverse
                y_next[step, way, lanes] = to_next
                y_link[step, way, lanes] = to_left
                y_inverse[step, way, lanes] = inverse
                left_excess[way] = left_excess[way] + to_left * excess[way]
                link[way] = to_left * face
                excess[way] = 1.0 + to_next * excess[way]
        matrix = [(link[way], excess[way], left_excess[way]) for way in range(WAYS)]
        joined = tree_matrix(matrix, y_coefs, lanes)
        for place, member in enumerate(joined):
            y_matrix_send[lanes, place : place + 1, :] = member[:, 0:1, :]

    def to_y_peers(source, target, send_sems, recv_sems):
        height = source.shape[1]
        copies = []
        for offset in range(1, count_y):
            slot = count_y - 1 - offset
            copies.append(
                pltpu.make_async_remote_copy(
                    src_ref=source,
                    dst_ref=target.at[:, pl.ds(SUB * slot, height), :],
                    send_sem=send_sems.at[slot],
                    recv_sem=recv_sems.at[slot],
                    device_id=peer_y(offset),
                    device_id_type=MESH,
                )
            )
            copies[-1].start()
        return copies

    matrix_copies = to_y_peers(y_matrix_send, y_matrix_recv, matrix_send_sems, matrix_recv_sems)

    spare = SUB * (count_y - 1)
    y_matrix_recv[:, spare : spare + 1, :] = jnp.full((blocks_y, 1, LANES), SHORT, jnp.float32)
    y_matrix_recv[:, spare + 1 : spare + 3, :] = jnp.zeros((blocks_y, 2, LANES), jnp.float32)
    y_source_recv[:, spare : spare + 2, :] = jnp.zeros((blocks_y, 2, LANES), jnp.float32)
    spread_coefs(x_coefs, every, row_x)
    spread_mids(x_mids, every, row_x)

    def load_block(ref):
        return (
            tuple(ref[:, place : place + 1, :] for place in range(3)),
            tuple(ref[:, place : place + 1, :] for place in range(3, 5)),
        )

    def join(low, high):
        matrix, coefs = join_matrix(low[0], high[0])
        source, _ = join_source(low[1], high[1], coefs)
        return matrix, source

    for offset in offsets:
        x_copies[-offset].wait_recv()
    near = {offset: load_block(x_recv.at[slot_of(offset)]) for offset in offsets}
    above = join(join(near[1], near[2]), join(near[3], near[4]))
    below_three = join(near[-3], join(near[-2], near[-1]))
    below = join(near[-4], below_three)
    pair_copies = []
    for place, (block, offset) in enumerate(((above, -REACH), (below_three, REACH))):
        for index, member in enumerate(block[0] + block[1]):
            x_pair_send[place, :, index : index + 1, :] = member
        pair_copies.append(
            pltpu.make_async_remote_copy(
                src_ref=x_pair_send.at[place],
                dst_ref=x_pair_recv.at[place],
                send_sem=pair_send_sems.at[place],
                recv_sem=pair_recv_sems.at[place],
                device_id=peer_x(offset),
                device_id_type=MESH,
            )
        )
        pair_copies[-1].start()

    for copy in matrix_copies:
        copy.wait_recv()
    rings = []
    for lanes in groups:
        blocks = [
            tuple(
                y_matrix_recv[lanes, pl.ds(SUB * way + place, SUB, stride=WAYS * SUB), :]
                for place in range(3)
            )
            for way in range(WAYS)
        ]
        rings.append(tree_matrix(blocks, ring_coefs, lanes))

    for copy in pair_copies:
        copy.wait_recv()
    far_above = load_block(x_pair_recv.at[0])
    far_below = load_block(x_pair_recv.at[1])
    rest = join(join(above, far_above), join(far_below, below))
    own = load_block(x_send)
    own_value, prev_value = solve_pair(own[0], own[1], rest[0], rest[1])

    nodes = tree_down(
        jnp.broadcast_to(prev_value, shape_x),
        jnp.broadcast_to(own_value, shape_x),
        x_coefs,
        x_mids,
        every,
        row_x,
    )
    values = list(nodes[1:])
    for way in range(WAYS):
        temp_turned[:, rows_of(way, length_x - 1, length_x), :] = values[way]
    for step in range(length_x - 2, -1, -1):
        for way in range(WAYS):
            values[way] = (x_mid[step, way] + x_link[step, way] * nodes[way]) + x_next[
                step, way
            ] * values[way]
            temp_turned[:, rows_of(way, step, length_x), :] = values[way]
    for block in range(blocks_x):
        for other in range(blocks_y):
            half_ref[other, LANES * block : LANES * (block + 1), :] = temp_turned[
                block, LANES * other : LANES * (other + 1), :
            ].T

    for lanes in groups:
        source = [half_ref[lanes, rows_of(way, 0, length_y), :] for way in range(WAYS)]
        left_source = [jnp.zeros(shape_y, jnp.float32)] * WAYS
        for step in range(length_y - 1):
            for way in range(WAYS):
                y_mid[step, way, lanes] = source[way] * y_inverse[step, way, lanes]
                left_source[way] = left_source[way] + y_link[step, way, lanes] * source[way]
                source[way] = (
                    half_ref[lanes, rows_of(way, step + 1, length_y), :]
                    + y_next[step, way, lanes] * source[way]
                )
        joined = tree_source(
            [(source[way], left_source[way]) for way in range(WAYS)], y_coefs, y_mids, lanes
        )
        for place, member in enumerate(joined):
            y_source_send[lanes, place : place + 1, :] = member[:, 0:1, :]
    source_copies = to_y_peers(y_source_send, y_source_recv, source_send_sems, source_recv_sems)
    for lanes in groups:
        spread_coefs(y_coefs, lanes, row_y)
        spread_mids(y_mids, lanes, row_y)
    for copy in source_copies:
        copy.wait_recv()

    stores = []
    for group, lanes in enumerate(groups):
        blocks = [
            tuple(
                y_source_recv[lanes, pl.ds(SUB * way + place, SUB, stride=WAYS * SUB), :]
                for place in range(2)
            )
            for way in range(WAYS)
        ]
        ring_source = tree_source(blocks, ring_coefs, ring_mids, lanes)
        own_value, prev_value = solve_pair(
            tuple(y_matrix_send[lanes, place : place + 1, :] for place in range(3)),
            tuple(y_source_send[lanes, place : place + 1, :] for place in range(2)),
            tuple(member[:, 0:1, :] for member in rings[group]),
            tuple(member[:, 0:1, :] for member in ring_source),
        )
        nodes = tree_down(
            jnp.broadcast_to(prev_value, shape_y),
            jnp.broadcast_to(own_value, shape_y),
            y_coefs,
            y_mids,
            lanes,
            row_y,
        )
        values = list(nodes[1:])
        for way in range(WAYS):
            half_ref[lanes, rows_of(way, length_y - 1, length_y), :] = values[way]
        for step in range(length_y - 2, -1, -1):
            for way in range(WAYS):
                values[way] = (
                    y_mid[step, way, lanes] + y_link[step, way, lanes] * nodes[way]
                ) + y_next[step, way, lanes] * values[way]
                half_ref[lanes, rows_of(way, step, length_y), :] = values[way]
        for block in range(lanes.start, lanes.stop):
            stores.append(
                pltpu.make_async_copy(
                    half_ref.at[block],
                    out_hbm.at[:, pl.ds(LANES * block, LANES)],
                    out_sems.at[block],
                )
            )
            stores[-1].start()

    for copy in x_copies.values():
        copy.wait_send()
    for copy in pair_copies + matrix_copies + source_copies:
        copy.wait_send()
    for store in stores:
        store.wait()


def body(initial_temp, kx_low, ky_low):
    count_x = lax.axis_size("gx")
    count_y = lax.axis_size("gy")
    _, rows, columns = initial_temp.shape
    length_x = columns // (WAYS * SUB)
    length_y = rows // (WAYS * SUB)
    blocks_x = rows // LANES
    blocks_y = columns // LANES

    def vmem(*shape):
        return pltpu.VMEM(shape, jnp.float32)

    def sems(*shape):
        return pltpu.SemaphoreType.DMA(shape)

    result = pl.pallas_call(
        functools.partial(kernel, count_x, count_y),
        out_shape=jax.ShapeDtypeStruct((rows, columns), jnp.float32),
        in_specs=[pl.BlockSpec(memory_space=pl.ANY)] * 3,
        out_specs=pl.BlockSpec(memory_space=pl.ANY),
        scratch_shapes=[
            vmem(rows, columns),
            vmem(rows, columns),
            vmem(blocks_y, rows, LANES),
            vmem(blocks_x, columns, LANES),
            vmem(blocks_x, columns, LANES),
            vmem(blocks_y, rows, LANES),
            vmem(length_x - 1, WAYS, blocks_x, SUB, LANES),
            vmem(length_x - 1, WAYS, blocks_x, SUB, LANES),
            vmem(length_x - 1, WAYS, blocks_x, SUB, LANES),
            vmem(length_y - 1, WAYS, blocks_y, SUB, LANES),
            vmem(length_y - 1, WAYS, blocks_y, SUB, LANES),
            vmem(length_y - 1, WAYS, blocks_y, SUB, LANES),
            vmem(length_y - 1, WAYS, blocks_y, SUB, LANES),
            vmem(18, blocks_x, SUB, LANES),
            vmem(6, blocks_x, SUB, LANES),
            vmem(18, blocks_y, SUB, LANES),
            vmem(6, blocks_y, SUB, LANES),
            vmem(18, blocks_y, SUB, LANES),
            vmem(6, blocks_y, SUB, LANES),
            vmem(blocks_x, 5, LANES),
            vmem(2, blocks_x, 5, LANES),
            vmem(2 * REACH, blocks_x, 5, LANES),
            vmem(2, blocks_x, 5, LANES),
            vmem(blocks_y, 3, LANES),
            vmem(blocks_y, count_y * SUB, LANES),
            vmem(blocks_y, 2, LANES),
            vmem(blocks_y, count_y * SUB, LANES),
            sems(2 + blocks_y),
            sems(blocks_y),
            sems(2 * REACH),
            sems(2 * REACH),
            sems(2),
            sems(2),
            sems(count_y - 1),
            sems(count_y - 1),
            sems(count_y - 1),
            sems(count_y - 1),
        ],
        compiler_params=pltpu.CompilerParams(collective_id=0, has_side_effects=True),
    )(initial_temp[0], kx_low[0], ky_low[0])
    return result[None]


def solution(mesh):
    spec = P(None, "gy", "gx")
    return jax.shard_map(
        body, mesh=mesh, in_specs=(spec, spec, spec), out_specs=spec, check_vma=False
    )
```

```python
import functools

import jax
import jax.numpy as jnp
from jax import lax
from jax.experimental import pallas as pl
from jax.experimental.pallas import tpu as pltpu
from jax.sharding import PartitionSpec as P

MESH = pl.DeviceIdType.MESH
SUB = 8
LANES = 128
WAYS = 4
REACH = 4
SHORT = 1e30
SLOT_RUN = 36
ROOM = 24 * 1024 * 1024
SMALL_ROOM = 1024 * 1024


def recip(value):
    return pltpu.reciprocal(value, full_range=False)


def join_matrix(low, high):
    excess = low[1] + high[2]
    inverse = recip(excess + (low[0] + high[0]))
    to_low = low[0] * inverse
    to_high = high[0] * inverse
    joined = (to_low * high[0], high[1] + to_high * excess, low[2] + to_low * excess)
    return joined, (inverse, to_low, to_high)


def join_source(low, high, coefs):
    inverse, to_low, to_high = coefs
    source = low[0] + high[1]
    return (high[0] + to_high * source, low[1] + to_low * source), source * inverse


def next_rows(value, steps):
    return pltpu.roll(value, SUB - steps, 1)


def tree_matrix(blocks, coef_ref, lanes):
    def keep(slot, coefs):
        for place, coef in enumerate(coefs):
            coef_ref[3 * slot + place, lanes] = coef

    first, coefs = join_matrix(blocks[0], blocks[1])
    keep(0, coefs)
    second, coefs = join_matrix(blocks[2], blocks[3])
    keep(1, coefs)
    joined, coefs = join_matrix(first, second)
    keep(2, coefs)
    for level in range(3):
        other = tuple(next_rows(member, 1 << level) for member in joined)
        joined, coefs = join_matrix(joined, other)
        keep(3 + level, coefs)
    return joined


def tree_source(blocks, coef_ref, mid_ref, lanes):
    def coefs(slot):
        return tuple(coef_ref[3 * slot + place, lanes] for place in range(3))

    first, mid = join_source(blocks[0], blocks[1], coefs(0))
    mid_ref[0, lanes] = mid
    second, mid = join_source(blocks[2], blocks[3], coefs(1))
    mid_ref[1, lanes] = mid
    joined, mid = join_source(first, second, coefs(2))
    mid_ref[2, lanes] = mid
    for level in range(3):
        other = tuple(next_rows(member, 1 << level) for member in joined)
        joined, mid = join_source(joined, other, coefs(3 + level))
        mid_ref[3 + level, lanes] = mid
    return joined


def spread(value, level, row):
    for bit in range(level + 1):
        value = jnp.where((row & (1 << bit)) != 0, pltpu.roll(value, 1 << bit, 1), value)
    return value


def spread_coefs(coef_ref, lanes, row):
    for level in range(3):
        for place in (1, 2):
            slot = 3 * (3 + level) + place
            coef_ref[slot, lanes] = spread(coef_ref[slot, lanes], level, row)


def spread_mids(mid_ref, lanes, row):
    for level in range(3):
        mid_ref[3 + level, lanes] = spread(mid_ref[3 + level, lanes], level, row)


def tree_down(left, right, coef_ref, mid_ref, lanes, row):
    def middle(slot, low, high):
        value = coef_ref[3 * slot + 1, lanes] * low + coef_ref[3 * slot + 2, lanes] * high
        return value if mid_ref is None else mid_ref[slot, lanes] + value

    for level in (2, 1, 0):
        mid = middle(3 + level, left, right)
        lower = (row & (1 << level)) == 0
        left, right = jnp.where(lower, left, mid), jnp.where(lower, mid, right)
    center = middle(2, left, right)
    lower_mid = middle(0, left, center)
    upper_mid = middle(1, center, right)
    return (left, lower_mid, center, upper_mid, right)


def solve_pair(own_matrix, own_source, rest_matrix, rest_source):
    link = own_matrix[0] + rest_matrix[0]
    own_excess = own_matrix[1] + rest_matrix[2]
    prev_excess = own_matrix[2] + rest_matrix[1]
    own_total = own_source[0] + rest_source[1]
    prev_total = own_source[1] + rest_source[0]
    inverse = recip(own_excess * prev_excess + link * (own_excess + prev_excess))
    both = link * (own_total + prev_total)
    own_value = (own_total * prev_excess + both) * inverse
    prev_value = (prev_total * own_excess + both) * inverse
    return own_value, prev_value


def kernel(
    count_x,
    count_y,
    temp_hbm,
    kx_hbm,
    ky_hbm,
    out_ref,
    temp_ref,
    kx_ref,
    ky_flat,
    ky_ref,
    temp_turned,
    kx_turned,
    third_turned,
    local_field,
    left_field,
    right_field,
    own_column,
    prev_column,
    x_link,
    x_next,
    x_mid,
    y_link,
    y_next,
    y_inverse,
    y_mid,
    x_coefs,
    x_mids,
    y_coefs,
    y_mids,
    ring_coefs,
    ring_mids,
    x_send,
    x_pair_send,
    x_recv,
    x_pair_recv,
    y_matrix_send,
    y_matrix_recv,
    y_source_send,
    y_source_recv,
    in_sems,
    x_send_sems,
    x_recv_sems,
    pair_send_sems,
    pair_recv_sems,
    matrix_send_sems,
    matrix_recv_sems,
    source_send_sems,
    source_recv_sems,
):
    rows, columns = temp_ref.shape
    blocks_x = rows // LANES
    blocks_y = columns // LANES
    my_x = lax.axis_index("gx")
    my_y = lax.axis_index("gy")
    loads = [
        pltpu.make_async_copy(kx_hbm, kx_ref, in_sems.at[0]),
        pltpu.make_async_copy(temp_hbm, temp_ref, in_sems.at[1]),
        pltpu.make_async_copy(ky_hbm, ky_flat, in_sems.at[2]),
    ]
    for load in loads:
        load.start()

    def peer_x(offset):
        return {"gx": lax.rem(my_x + (offset + count_x), count_x)}

    def peer_y(offset):
        return {"gy": lax.rem(my_y + offset, count_y)}

    offsets = [sign * step for step in range(REACH, 0, -1) for sign in (1, -1)]
    barrier = pltpu.get_barrier_semaphore()
    for offset in offsets:
        pl.semaphore_signal(barrier, inc=1, device_id=peer_x(offset), device_id_type=MESH)
    for offset in range(1, count_y):
        pl.semaphore_signal(barrier, inc=1, device_id=peer_y(offset), device_id_type=MESH)

    def slot_of(offset):
        return offset + REACH - (1 if offset > 0 else 0)

    shape_x = (blocks_x, SUB, LANES)
    row_x = lax.broadcasted_iota(jnp.int32, shape_x, 1)
    every = slice(0, blocks_x)
    length_x = columns // (WAYS * SUB)
    length_y = rows // (WAYS * SUB)

    def rows_of(way, step, length):
        return pl.ds(way * length + step, SUB, stride=WAYS * length + 1)

    def put(target, first, values, length):
        run = WAYS * length
        for top in range(0, values.shape[0], min(run, values.shape[0])):
            place = first + top
            target[pl.ds(place + place // run, min(run, values.shape[0])), :] = values[
                top : top + min(run, values.shape[0])
            ]

    def turn_in(source, target):
        for block in range(blocks_x):
            for left in range(0, columns, LANES):
                put(
                    target.at[block],
                    left,
                    source[LANES * block : LANES * (block + 1), left : left + LANES].T,
                    length_x,
                )

    loads[0].wait()
    turn_in(kx_ref, kx_turned)
    loads[1].wait()
    turn_in(temp_ref, temp_turned)

    excess = [jnp.ones(shape_x, jnp.float32)] * WAYS
    link = [kx_turned[:, rows_of(way, 0, length_x), :] for way in range(WAYS)]
    source = [temp_turned[:, rows_of(way, 0, length_x), :] for way in range(WAYS)]
    left_excess = [jnp.zeros(shape_x, jnp.float32)] * WAYS
    left_source = [jnp.zeros(shape_x, jnp.float32)] * WAYS
    for step in range(length_x - 1):
        for way in range(WAYS):
            face = kx_turned[:, rows_of(way, step + 1, length_x), :]
            inverse = recip(excess[way] + link[way] + face)
            to_next = face * inverse
            to_left = link[way] * inverse
            x_next[step, way] = to_next
            x_link[step, way] = to_left
            x_mid[step, way] = source[way] * inverse
            left_excess[way] = left_excess[way] + to_left * excess[way]
            left_source[way] = left_source[way] + to_left * source[way]
            link[way] = to_left * face
            excess[way] = 1.0 + to_next * excess[way]
            source[way] = (
                temp_turned[:, rows_of(way, step + 1, length_x), :] + to_next * source[way]
            )
    matrix = [(link[way], excess[way], left_excess[way]) for way in range(WAYS)]
    own_matrix = tree_matrix(matrix, x_coefs, every)
    own_source = tree_source(
        [(source[way], left_source[way]) for way in range(WAYS)], x_coefs, x_mids, every
    )
    for place, member in enumerate(own_matrix + own_source):
        x_send[:, place : place + 1, :] = member[:, 0:1, :]

    pl.semaphore_wait(barrier, len(offsets) + count_y - 1)

    x_copies = {}
    for offset in offsets:
        x_copies[offset] = pltpu.make_async_remote_copy(
            src_ref=x_send,
            dst_ref=x_recv.at[slot_of(-offset)],
            send_sem=x_send_sems.at[slot_of(offset)],
            recv_sem=x_recv_sems.at[slot_of(-offset)],
            device_id=peer_x(offset),
            device_id_type=MESH,
        )
        x_copies[offset].start()

    loads[2].wait()
    for block in range(blocks_y):
        put(ky_ref.at[block], 0, ky_flat[:, LANES * block : LANES * (block + 1)], length_y)
    width = 2
    shape_y = (width, SUB, LANES)
    groups = [slice(start, start + width) for start in range(0, blocks_y, width)]
    row_y = lax.broadcasted_iota(jnp.int32, shape_y, 1)
    for lanes in groups:
        excess = [jnp.ones(shape_y, jnp.float32)] * WAYS
        link = [ky_ref[lanes, rows_of(way, 0, length_y), :] for way in range(WAYS)]
        left_excess = [jnp.zeros(shape_y, jnp.float32)] * WAYS
        for step in range(length_y - 1):
            for way in range(WAYS):
                face = ky_ref[lanes, rows_of(way, step + 1, length_y), :]
                inverse = recip(excess[way] + link[way] + face)
                to_next = face * inverse
                to_left = link[way] * inverse
                y_next[step, way, lanes] = to_next
                y_link[step, way, lanes] = to_left
                y_inverse[step, way, lanes] = inverse
                left_excess[way] = left_excess[way] + to_left * excess[way]
                link[way] = to_left * face
                excess[way] = 1.0 + to_next * excess[way]
        matrix = [(link[way], excess[way], left_excess[way]) for way in range(WAYS)]
        joined = tree_matrix(matrix, y_coefs, lanes)
        for place, member in enumerate(joined):
            y_matrix_send[lanes, place : place + 1, :] = member[:, 0:1, :]

    def row_of_slot(slot):
        return SLOT_RUN * (slot // WAYS) + SUB * (slot % WAYS)

    def to_y_peers(source, target, send_sems, recv_sems):
        height = source.shape[1]
        copies = []
        for offset in range(1, count_y):
            slot = count_y - 1 - offset
            copies.append(
                pltpu.make_async_remote_copy(
                    src_ref=source,
                    dst_ref=target.at[:, pl.ds(row_of_slot(slot), height), :],
                    send_sem=send_sems.at[slot],
                    recv_sem=recv_sems.at[slot],
                    device_id=peer_y(offset),
                    device_id_type=MESH,
                )
            )
            copies[-1].start()
        return copies

    matrix_copies = to_y_peers(y_matrix_send, y_matrix_recv, matrix_send_sems, matrix_recv_sems)

    spare = row_of_slot(count_y - 1)
    y_matrix_recv[:, spare : spare + 1, :] = jnp.full((blocks_y, 1, LANES), SHORT, jnp.float32)
    y_matrix_recv[:, spare + 1 : spare + 3, :] = jnp.zeros((blocks_y, 2, LANES), jnp.float32)
    y_source_recv[:, spare : spare + 2, :] = jnp.zeros((blocks_y, 2, LANES), jnp.float32)
    spread_coefs(x_coefs, every, row_x)
    spread_mids(x_mids, every, row_x)

    zeros = jnp.zeros(shape_x, jnp.float32)
    ones = jnp.ones(shape_x, jnp.float32)
    for left, right, mids, cells, turned, field in (
        (zeros, zeros, x_mids, x_mid, temp_turned, local_field),
        (ones, zeros, None, None, kx_turned, left_field),
        (zeros, ones, None, None, third_turned, right_field),
    ):
        nodes = tree_down(left, right, x_coefs, mids, every, row_x)
        values = list(nodes[1:])
        for way in range(WAYS):
            turned[:, rows_of(way, length_x - 1, length_x), :] = values[way]
        for step in range(length_x - 2, -1, -1):
            for way in range(WAYS):
                value = x_link[step, way] * nodes[way] + x_next[step, way] * values[way]
                values[way] = value if cells is None else cells[step, way] + value
                turned[:, rows_of(way, step, length_x), :] = values[way]
        for block in range(blocks_x):
            for other in range(blocks_y):
                run = WAYS * length_x
                parts = [
                    turned[block, pl.ds(place + place // run, run), :]
                    for place in range(LANES * other, LANES * (other + 1), run)
                ]
                put(field.at[other], LANES * block, jnp.concatenate(parts, axis=0).T, length_y)

    def load_block(ref):
        return (
            tuple(ref[:, place : place + 1, :] for place in range(3)),
            tuple(ref[:, place : place + 1, :] for place in range(3, 5)),
        )

    def join(low, high):
        matrix, coefs = join_matrix(low[0], high[0])
        source, _ = join_source(low[1], high[1], coefs)
        return matrix, source

    for offset in offsets:
        x_copies[-offset].wait_recv()
    near = {offset: load_block(x_recv.at[slot_of(offset)]) for offset in offsets}
    above = join(join(near[1], near[2]), join(near[3], near[4]))
    below_three = join(near[-3], join(near[-2], near[-1]))
    below = join(near[-4], below_three)
    pair_copies = []
    for place, (block, offset) in enumerate(((above, -REACH), (below_three, REACH))):
        for index, member in enumerate(block[0] + block[1]):
            x_pair_send[place, :, index : index + 1, :] = member
        pair_copies.append(
            pltpu.make_async_remote_copy(
                src_ref=x_pair_send.at[place],
                dst_ref=x_pair_recv.at[place],
                send_sem=pair_send_sems.at[place],
                recv_sem=pair_recv_sems.at[place],
                device_id=peer_x(offset),
                device_id_type=MESH,
            )
        )
        pair_copies[-1].start()

    for copy in matrix_copies:
        copy.wait_recv()
    rings = []
    for lanes in groups:
        blocks = [
            tuple(
                y_matrix_recv[lanes, pl.ds(SUB * way + place, SUB, stride=SLOT_RUN), :]
                for place in range(3)
            )
            for way in range(WAYS)
        ]
        rings.append(tree_matrix(blocks, ring_coefs, lanes))

    for copy in pair_copies:
        copy.wait_recv()
    far_above = load_block(x_pair_recv.at[0])
    far_below = load_block(x_pair_recv.at[1])
    rest = join(join(above, far_above), join(far_below, below))
    own = load_block(x_send)
    own_value, prev_value = solve_pair(own[0], own[1], rest[0], rest[1])

    for value, column in ((own_value, own_column), (prev_value, prev_column)):
        for block in range(blocks_x):
            put(column, LANES * block, jnp.broadcast_to(value[block], (LANES, LANES)).T, length_y)

    def half_rows(lanes, way, step):
        rows_here = rows_of(way, step, length_y)
        return (
            local_field[lanes, rows_here, :]
            + prev_column[rows_here, :] * left_field[lanes, rows_here, :]
            + own_column[rows_here, :] * right_field[lanes, rows_here, :]
        )

    for lanes in groups:
        source = [half_rows(lanes, way, 0) for way in range(WAYS)]
        left_source = [jnp.zeros(shape_y, jnp.float32)] * WAYS
        for step in range(length_y - 1):
            for way in range(WAYS):
                y_mid[step, way, lanes] = source[way] * y_inverse[step, way, lanes]
                left_source[way] = left_source[way] + y_link[step, way, lanes] * source[way]
                source[way] = (
                    half_rows(lanes, way, step + 1)
                    + y_next[step, way, lanes] * source[way]
                )
        joined = tree_source(
            [(source[way], left_source[way]) for way in range(WAYS)], y_coefs, y_mids, lanes
        )
        for place, member in enumerate(joined):
            y_source_send[lanes, place : place + 1, :] = member[:, 0:1, :]
    source_copies = to_y_peers(y_source_send, y_source_recv, source_send_sems, source_recv_sems)
    for lanes in groups:
        spread_coefs(y_coefs, lanes, row_y)
        spread_mids(y_mids, lanes, row_y)
    for copy in source_copies:
        copy.wait_recv()

    for group, lanes in enumerate(groups):
        blocks = [
            tuple(
                y_source_recv[lanes, pl.ds(SUB * way + place, SUB, stride=SLOT_RUN), :]
                for place in range(2)
            )
            for way in range(WAYS)
        ]
        ring_source = tree_source(blocks, ring_coefs, ring_mids, lanes)
        own_value, prev_value = solve_pair(
            tuple(y_matrix_send[lanes, place : place + 1, :] for place in range(3)),
            tuple(y_source_send[lanes, place : place + 1, :] for place in range(2)),
            tuple(member[:, 0:1, :] for member in rings[group]),
            tuple(member[:, 0:1, :] for member in ring_source),
        )
        nodes = tree_down(
            jnp.broadcast_to(prev_value, shape_y),
            jnp.broadcast_to(own_value, shape_y),
            y_coefs,
            y_mids,
            lanes,
            row_y,
        )
        values = list(nodes[1:])
        for way in range(WAYS):
            out_ref[lanes, rows_of(way, length_y - 1, length_y), :] = values[way]
        for step in range(length_y - 2, -1, -1):
            for way in range(WAYS):
                values[way] = (
                    y_mid[step, way, lanes] + y_link[step, way, lanes] * nodes[way]
                ) + y_next[step, way, lanes] * values[way]
                out_ref[lanes, rows_of(way, step, length_y), :] = values[way]

    for copy in x_copies.values():
        copy.wait_send()
    for copy in pair_copies + matrix_copies + source_copies:
        copy.wait_send()


def put_out(blocks_ref, out_hbm, sems):
    run = out_hbm.shape[0] // SUB
    stores = [
        pltpu.make_async_copy(
            blocks_ref.at[block, pl.ds((run + 1) * part, run)],
            out_hbm.at[pl.ds(run * part, run), pl.ds(LANES * block, LANES)],
            sems.at[block, part],
        )
        for block in range(blocks_ref.shape[0])
        for part in range(SUB)
    ]
    for store in stores:
        store.start()
    for store in stores:
        store.wait()


def body(initial_temp, kx_low, ky_low):
    count_x = lax.axis_size("gx")
    count_y = lax.axis_size("gy")
    _, rows, columns = initial_temp.shape
    length_x = columns // (WAYS * SUB)
    length_y = rows // (WAYS * SUB)
    blocks_x = rows // LANES
    blocks_y = columns // LANES

    def vmem(*shape):
        return pltpu.VMEM(shape, jnp.float32)

    def sems(*shape):
        return pltpu.SemaphoreType.DMA(shape)

    blocks = pl.pallas_call(
        functools.partial(kernel, count_x, count_y),
        out_shape=jax.ShapeDtypeStruct((blocks_y, rows + SUB, LANES), jnp.float32),
        in_specs=[pl.BlockSpec(memory_space=pltpu.HBM)] * 3,
        out_specs=pl.BlockSpec(memory_space=pltpu.VMEM),
        scratch_shapes=[
            vmem(rows, columns),
            vmem(rows, columns),
            vmem(rows, columns),
            vmem(blocks_y, rows + SUB, LANES),
            vmem(blocks_x, columns + SUB, LANES),
            vmem(blocks_x, columns + SUB, LANES),
            vmem(blocks_x, columns + SUB, LANES),
            vmem(blocks_y, rows + SUB, LANES),
            vmem(blocks_y, rows + SUB, LANES),
            vmem(blocks_y, rows + SUB, LANES),
            vmem(rows + SUB, LANES),
            vmem(rows + SUB, LANES),
            vmem(length_x - 1, WAYS, blocks_x, SUB, LANES),
            vmem(length_x - 1, WAYS, blocks_x, SUB, LANES),
            vmem(length_x - 1, WAYS, blocks_x, SUB, LANES),
            vmem(length_y - 1, WAYS, blocks_y, SUB, LANES),
            vmem(length_y - 1, WAYS, blocks_y, SUB, LANES),
            vmem(length_y - 1, WAYS, blocks_y, SUB, LANES),
            vmem(length_y - 1, WAYS, blocks_y, SUB, LANES),
            vmem(18, blocks_x, SUB, LANES),
            vmem(6, blocks_x, SUB, LANES),
            vmem(18, blocks_y, SUB, LANES),
            vmem(6, blocks_y, SUB, LANES),
            vmem(18, blocks_y, SUB, LANES),
            vmem(6, blocks_y, SUB, LANES),
            vmem(blocks_x, 5, LANES),
            vmem(2, blocks_x, 5, LANES),
            vmem(2 * REACH, blocks_x, 5, LANES),
            vmem(2, blocks_x, 5, LANES),
            vmem(blocks_y, 3, LANES),
            vmem(blocks_y, SUB * SLOT_RUN, LANES),
            vmem(blocks_y, 2, LANES),
            vmem(blocks_y, SUB * SLOT_RUN, LANES),
            sems(3),
            sems(2 * REACH),
            sems(2 * REACH),
            sems(2),
            sems(2),
            sems(count_y - 1),
            sems(count_y - 1),
            sems(count_y - 1),
            sems(count_y - 1),
        ],
        compiler_params=pltpu.CompilerParams(
            collective_id=0, has_side_effects=True, vmem_limit_bytes=ROOM
        ),
    )(*(pltpu.with_memory_space_constraint(value[0], pltpu.HBM) for value in (initial_temp, kx_low, ky_low)))
    result = pl.pallas_call(
        put_out,
        out_shape=jax.ShapeDtypeStruct((rows, columns), jnp.float32),
        in_specs=[pl.BlockSpec(memory_space=pltpu.VMEM)],
        out_specs=pl.BlockSpec(memory_space=pltpu.HBM),
        scratch_shapes=[sems(blocks_y, SUB)],
        compiler_params=pltpu.CompilerParams(vmem_limit_bytes=SMALL_ROOM),
    )(blocks)
    return result[None]


def solution(mesh):
    spec = P(None, "gy", "gx")
    return jax.shard_map(
        body, mesh=mesh, in_specs=(spec, spec, spec), out_specs=spec, check_vma=False
    )
```

```python
import functools

import jax
import jax.numpy as jnp
from jax import lax
from jax.experimental import pallas as pl
from jax.experimental.pallas import tpu as pltpu
from jax.sharding import PartitionSpec as P

MESH = pl.DeviceIdType.MESH
SUB = 8
LANES = 128
WAYS = 4
REACH = 4
SHORT = 1e30
RING = 4
SLOT_RUN = 36
ROOM = 24 * 1024 * 1024
SMALL_ROOM = 1024 * 1024


def recip(value):
    return pltpu.reciprocal(value, full_range=False)


def join_matrix(low, high):
    excess = low[1] + high[2]
    inverse = recip(excess + (low[0] + high[0]))
    to_low = low[0] * inverse
    to_high = high[0] * inverse
    joined = (to_low * high[0], high[1] + to_high * excess, low[2] + to_low * excess)
    return joined, (inverse, to_low, to_high)


def join_source(low, high, coefs):
    inverse, to_low, to_high = coefs
    source = low[0] + high[1]
    return (high[0] + to_high * source, low[1] + to_low * source), source * inverse


def next_rows(value, steps):
    return pltpu.roll(value, SUB - steps, 1)


def tree_matrix(blocks, coef_ref, lanes):
    def keep(slot, coefs):
        for place, coef in enumerate(coefs):
            coef_ref[3 * slot + place, lanes] = coef

    first, coefs = join_matrix(blocks[0], blocks[1])
    keep(0, coefs)
    second, coefs = join_matrix(blocks[2], blocks[3])
    keep(1, coefs)
    joined, coefs = join_matrix(first, second)
    keep(2, coefs)
    for level in range(3):
        other = tuple(next_rows(member, 1 << level) for member in joined)
        joined, coefs = join_matrix(joined, other)
        keep(3 + level, coefs)
    return joined


def tree_source(blocks, coef_ref, mid_ref, lanes):
    def coefs(slot):
        return tuple(coef_ref[3 * slot + place, lanes] for place in range(3))

    first, mid = join_source(blocks[0], blocks[1], coefs(0))
    mid_ref[0, lanes] = mid
    second, mid = join_source(blocks[2], blocks[3], coefs(1))
    mid_ref[1, lanes] = mid
    joined, mid = join_source(first, second, coefs(2))
    mid_ref[2, lanes] = mid
    for level in range(3):
        other = tuple(next_rows(member, 1 << level) for member in joined)
        joined, mid = join_source(joined, other, coefs(3 + level))
        mid_ref[3 + level, lanes] = mid
    return joined


def spread(value, level, row):
    for bit in range(level + 1):
        value = jnp.where((row & (1 << bit)) != 0, pltpu.roll(value, 1 << bit, 1), value)
    return value


def spread_coefs(coef_ref, lanes, row):
    for level in range(3):
        for place in (1, 2):
            slot = 3 * (3 + level) + place
            coef_ref[slot, lanes] = spread(coef_ref[slot, lanes], level, row)


def spread_mids(mid_ref, lanes, row):
    for level in range(3):
        mid_ref[3 + level, lanes] = spread(mid_ref[3 + level, lanes], level, row)


def tree_down(left, right, coef_ref, mid_ref, lanes, row):
    def middle(slot, low, high):
        value = coef_ref[3 * slot + 1, lanes] * low + coef_ref[3 * slot + 2, lanes] * high
        return value if mid_ref is None else mid_ref[slot, lanes] + value

    for level in (2, 1, 0):
        mid = middle(3 + level, left, right)
        lower = (row & (1 << level)) == 0
        left, right = jnp.where(lower, left, mid), jnp.where(lower, mid, right)
    center = middle(2, left, right)
    lower_mid = middle(0, left, center)
    upper_mid = middle(1, center, right)
    return (left, lower_mid, center, upper_mid, right)


def solve_pair(own_matrix, own_source, rest_matrix, rest_source):
    link = own_matrix[0] + rest_matrix[0]
    own_excess = own_matrix[1] + rest_matrix[2]
    prev_excess = own_matrix[2] + rest_matrix[1]
    own_total = own_source[0] + rest_source[1]
    prev_total = own_source[1] + rest_source[0]
    inverse = recip(own_excess * prev_excess + link * (own_excess + prev_excess))
    both = link * (own_total + prev_total)
    own_value = (own_total * prev_excess + both) * inverse
    prev_value = (prev_total * own_excess + both) * inverse
    return own_value, prev_value


def kernel(
    count_x,
    count_y,
    temp_hbm,
    kx_hbm,
    ky_hbm,
    out_ref,
    temp_ref,
    kx_ref,
    ky_flat,
    ky_ref,
    temp_turned,
    kx_turned,
    third_turned,
    local_field,
    left_field,
    right_field,
    own_column,
    prev_column,
    x_link,
    x_next,
    x_mid,
    y_link,
    y_next,
    y_inverse,
    y_mid,
    x_coefs,
    x_mids,
    y_coefs,
    y_mids,
    ring_coefs,
    ring_mids,
    x_send,
    x_pair_send,
    x_recv,
    x_pair_recv,
    y_matrix_send,
    y_matrix_recv,
    y_source_send,
    y_source_recv,
    in_sems,
    x_send_sem,
    x_recv_sem,
    pair_send_sem,
    pair_recv_sem,
    matrix_send_sem,
    matrix_recv_sem,
    source_send_sem,
    source_recv_sem,
):
    rows, columns = temp_ref.shape
    blocks_x = rows // LANES
    blocks_y = columns // LANES
    my_x = lax.axis_index("gx")
    my_y = lax.axis_index("gy")
    loads = [
        pltpu.make_async_copy(kx_hbm, kx_ref, in_sems.at[0]),
        pltpu.make_async_copy(temp_hbm, temp_ref, in_sems.at[1]),
        pltpu.make_async_copy(ky_hbm, ky_flat, in_sems.at[2]),
    ]
    for load in loads:
        load.start()

    def peer_x(offset):
        return {"gx": lax.rem(my_x + (offset + count_x), count_x)}

    def peer_y(offset):
        return {"gy": lax.rem(my_y + offset, count_y)}

    offsets = [sign * step for step in range(REACH, 0, -1) for sign in (1, -1)]

    def hops_y(offset):
        ring = offset // 2 // RING % RING
        place = offset // 2 % RING
        return min(ring, RING - ring) + min(place, RING - place)

    offsets_y = sorted(range(1, count_y), key=lambda offset: -hops_y(offset))
    barrier = pltpu.get_barrier_semaphore()
    for steps in range(REACH, -1, -1):
        for offset in offsets:
            if abs(offset) == steps:
                pl.semaphore_signal(
                    barrier, inc=1, device_id=peer_x(offset), device_id_type=MESH
                )
        for offset in offsets_y:
            if min(REACH, hops_y(offset)) == steps:
                pl.semaphore_signal(
                    barrier, inc=1, device_id=peer_y(offset), device_id_type=MESH
                )

    def slot_of(offset):
        return offset + REACH - (1 if offset > 0 else 0)

    shape_x = (blocks_x, SUB, LANES)
    row_x = lax.broadcasted_iota(jnp.int32, shape_x, 1)
    every = slice(0, blocks_x)
    length_x = columns // (WAYS * SUB)
    length_y = rows // (WAYS * SUB)

    def rows_of(way, step, length):
        return pl.ds(way * length + step, SUB, stride=WAYS * length + 1)

    def put(target, first, values, length):
        run = WAYS * length
        for top in range(0, values.shape[0], min(run, values.shape[0])):
            place = first + top
            target[pl.ds(place + place // run, min(run, values.shape[0])), :] = values[
                top : top + min(run, values.shape[0])
            ]

    def turn_in(source, target):
        for block in range(blocks_x):
            for left in range(0, columns, LANES):
                put(
                    target.at[block],
                    left,
                    source[LANES * block : LANES * (block + 1), left : left + LANES].T,
                    length_x,
                )

    loads[0].wait()
    turn_in(kx_ref, kx_turned)
    loads[1].wait()
    turn_in(temp_ref, temp_turned)

    excess = [jnp.ones(shape_x, jnp.float32)] * WAYS
    link = [kx_turned[:, rows_of(way, 0, length_x), :] for way in range(WAYS)]
    source = [temp_turned[:, rows_of(way, 0, length_x), :] for way in range(WAYS)]
    left_excess = [jnp.zeros(shape_x, jnp.float32)] * WAYS
    left_source = [jnp.zeros(shape_x, jnp.float32)] * WAYS
    for step in range(length_x - 1):
        for way in range(WAYS):
            face = kx_turned[:, rows_of(way, step + 1, length_x), :]
            inverse = recip(excess[way] + link[way] + face)
            to_next = face * inverse
            to_left = link[way] * inverse
            x_next[step, way] = to_next
            x_link[step, way] = to_left
            x_mid[step, way] = source[way] * inverse
            left_excess[way] = left_excess[way] + to_left * excess[way]
            left_source[way] = left_source[way] + to_left * source[way]
            link[way] = to_left * face
            excess[way] = 1.0 + to_next * excess[way]
            source[way] = (
                temp_turned[:, rows_of(way, step + 1, length_x), :] + to_next * source[way]
            )
    matrix = [(link[way], excess[way], left_excess[way]) for way in range(WAYS)]
    own_matrix = tree_matrix(matrix, x_coefs, every)
    own_source = tree_source(
        [(source[way], left_source[way]) for way in range(WAYS)], x_coefs, x_mids, every
    )
    for place, member in enumerate(own_matrix + own_source):
        x_send[:, place : place + 1, :] = member[:, 0:1, :]

    pl.semaphore_wait(barrier, len(offsets) + count_y - 1)

    for offset in offsets:
        pltpu.make_async_remote_copy(
            src_ref=x_send,
            dst_ref=x_recv.at[slot_of(-offset)],
            send_sem=x_send_sem,
            recv_sem=x_recv_sem,
            device_id=peer_x(offset),
            device_id_type=MESH,
        ).start()

    loads[2].wait()
    for block in range(blocks_y):
        put(ky_ref.at[block], 0, ky_flat[:, LANES * block : LANES * (block + 1)], length_y)
    width = 2
    shape_y = (width, SUB, LANES)
    groups = [slice(start, start + width) for start in range(0, blocks_y, width)]
    row_y = lax.broadcasted_iota(jnp.int32, shape_y, 1)
    for lanes in groups:
        excess = [jnp.ones(shape_y, jnp.float32)] * WAYS
        link = [ky_ref[lanes, rows_of(way, 0, length_y), :] for way in range(WAYS)]
        left_excess = [jnp.zeros(shape_y, jnp.float32)] * WAYS
        for step in range(length_y - 1):
            for way in range(WAYS):
                face = ky_ref[lanes, rows_of(way, step + 1, length_y), :]
                inverse = recip(excess[way] + link[way] + face)
                to_next = face * inverse
                to_left = link[way] * inverse
                y_next[step, way, lanes] = to_next
                y_link[step, way, lanes] = to_left
                y_inverse[step, way, lanes] = inverse
                left_excess[way] = left_excess[way] + to_left * excess[way]
                link[way] = to_left * face
                excess[way] = 1.0 + to_next * excess[way]
        matrix = [(link[way], excess[way], left_excess[way]) for way in range(WAYS)]
        joined = tree_matrix(matrix, y_coefs, lanes)
        for place, member in enumerate(joined):
            y_matrix_send[lanes, place : place + 1, :] = member[:, 0:1, :]

    def row_of_slot(slot):
        return SLOT_RUN * (slot // WAYS) + SUB * (slot % WAYS)

    def to_y_peers(source, target, send_sem, recv_sem):
        height = source.shape[1]
        for offset in offsets_y:
            slot = count_y - 1 - offset
            pltpu.make_async_remote_copy(
                src_ref=source,
                dst_ref=target.at[:, pl.ds(row_of_slot(slot), height), :],
                send_sem=send_sem,
                recv_sem=recv_sem,
                device_id=peer_y(offset),
                device_id_type=MESH,
            ).start()

    def all_peers(target, source):
        return target.at[:, pl.ds(0, source.shape[1] * (count_y - 1)), :]

    to_y_peers(y_matrix_send, y_matrix_recv, matrix_send_sem, matrix_recv_sem)

    spare = row_of_slot(count_y - 1)
    y_matrix_recv[:, spare : spare + 1, :] = jnp.full((blocks_y, 1, LANES), SHORT, jnp.float32)
    y_matrix_recv[:, spare + 1 : spare + 3, :] = jnp.zeros((blocks_y, 2, LANES), jnp.float32)
    y_source_recv[:, spare : spare + 2, :] = jnp.zeros((blocks_y, 2, LANES), jnp.float32)
    spread_coefs(x_coefs, every, row_x)
    spread_mids(x_mids, every, row_x)

    zeros = jnp.zeros(shape_x, jnp.float32)
    ones = jnp.ones(shape_x, jnp.float32)
    for left, right, mids, cells, turned, field in (
        (zeros, zeros, x_mids, x_mid, temp_turned, local_field),
        (ones, zeros, None, None, kx_turned, left_field),
        (zeros, ones, None, None, third_turned, right_field),
    ):
        nodes = tree_down(left, right, x_coefs, mids, every, row_x)
        values = list(nodes[1:])
        for way in range(WAYS):
            turned[:, rows_of(way, length_x - 1, length_x), :] = values[way]
        for step in range(length_x - 2, -1, -1):
            for way in range(WAYS):
                value = x_link[step, way] * nodes[way] + x_next[step, way] * values[way]
                values[way] = value if cells is None else cells[step, way] + value
                turned[:, rows_of(way, step, length_x), :] = values[way]
        for block in range(blocks_x):
            for other in range(blocks_y):
                run = WAYS * length_x
                parts = [
                    turned[block, pl.ds(place + place // run, run), :]
                    for place in range(LANES * other, LANES * (other + 1), run)
                ]
                put(field.at[other], LANES * block, jnp.concatenate(parts, axis=0).T, length_y)

    def load_block(ref):
        return (
            tuple(ref[:, place : place + 1, :] for place in range(3)),
            tuple(ref[:, place : place + 1, :] for place in range(3, 5)),
        )

    def join(low, high):
        matrix, coefs = join_matrix(low[0], high[0])
        source, _ = join_source(low[1], high[1], coefs)
        return matrix, source

    await_bytes(x_recv, x_recv_sem)
    near = {offset: load_block(x_recv.at[slot_of(offset)]) for offset in offsets}
    above = join(join(near[1], near[2]), join(near[3], near[4]))
    below_three = join(near[-3], join(near[-2], near[-1]))
    below = join(near[-4], below_three)
    for place, (block, offset) in enumerate(((above, -REACH), (below_three, REACH))):
        for index, member in enumerate(block[0] + block[1]):
            x_pair_send[place, :, index : index + 1, :] = member
        pltpu.make_async_remote_copy(
            src_ref=x_pair_send.at[place],
            dst_ref=x_pair_recv.at[place],
            send_sem=pair_send_sem,
            recv_sem=pair_recv_sem,
            device_id=peer_x(offset),
            device_id_type=MESH,
        ).start()

    await_bytes(all_peers(y_matrix_recv, y_matrix_send), matrix_recv_sem)
    rings = []
    for lanes in groups:
        blocks = [
            tuple(
                y_matrix_recv[lanes, pl.ds(SUB * way + place, SUB, stride=SLOT_RUN), :]
                for place in range(3)
            )
            for way in range(WAYS)
        ]
        rings.append(tree_matrix(blocks, ring_coefs, lanes))

    await_bytes(x_pair_recv, pair_recv_sem)
    far_above = load_block(x_pair_recv.at[0])
    far_below = load_block(x_pair_recv.at[1])
    rest = join(join(above, far_above), join(far_below, below))
    own = load_block(x_send)
    own_value, prev_value = solve_pair(own[0], own[1], rest[0], rest[1])

    for value, column in ((own_value, own_column), (prev_value, prev_column)):
        for block in range(blocks_x):
            put(column, LANES * block, jnp.broadcast_to(value[block], (LANES, LANES)).T, length_y)

    def half_rows(lanes, way, step):
        rows_here = rows_of(way, step, length_y)
        return (
            local_field[lanes, rows_here, :]
            + prev_column[rows_here, :] * left_field[lanes, rows_here, :]
            + own_column[rows_here, :] * right_field[lanes, rows_here, :]
        )

    for lanes in groups:
        source = [half_rows(lanes, way, 0) for way in range(WAYS)]
        left_source = [jnp.zeros(shape_y, jnp.float32)] * WAYS
        for step in range(length_y - 1):
            for way in range(WAYS):
                y_mid[step, way, lanes] = source[way] * y_inverse[step, way, lanes]
                left_source[way] = left_source[way] + y_link[step, way, lanes] * source[way]
                source[way] = (
                    half_rows(lanes, way, step + 1)
                    + y_next[step, way, lanes] * source[way]
                )
        joined = tree_source(
            [(source[way], left_source[way]) for way in range(WAYS)], y_coefs, y_mids, lanes
        )
        for place, member in enumerate(joined):
            y_source_send[lanes, place : place + 1, :] = member[:, 0:1, :]
    to_y_peers(y_source_send, y_source_recv, source_send_sem, source_recv_sem)
    for lanes in groups:
        spread_coefs(y_coefs, lanes, row_y)
        spread_mids(y_mids, lanes, row_y)
    await_bytes(all_peers(y_source_recv, y_source_send), source_recv_sem)

    for group, lanes in enumerate(groups):
        blocks = [
            tuple(
                y_source_recv[lanes, pl.ds(SUB * way + place, SUB, stride=SLOT_RUN), :]
                for place in range(2)
            )
            for way in range(WAYS)
        ]
        ring_source = tree_source(blocks, ring_coefs, ring_mids, lanes)
        own_value, prev_value = solve_pair(
            tuple(y_matrix_send[lanes, place : place + 1, :] for place in range(3)),
            tuple(y_source_send[lanes, place : place + 1, :] for place in range(2)),
            tuple(member[:, 0:1, :] for member in rings[group]),
            tuple(member[:, 0:1, :] for member in ring_source),
        )
        nodes = tree_down(
            jnp.broadcast_to(prev_value, shape_y),
            jnp.broadcast_to(own_value, shape_y),
            y_coefs,
            y_mids,
            lanes,
            row_y,
        )
        values = list(nodes[1:])
        for way in range(WAYS):
            out_ref[lanes, rows_of(way, length_y - 1, length_y), :] = values[way]
        for step in range(length_y - 2, -1, -1):
            for way in range(WAYS):
                values[way] = (
                    y_mid[step, way, lanes] + y_link[step, way, lanes] * nodes[way]
                ) + y_next[step, way, lanes] * values[way]
                out_ref[lanes, rows_of(way, step, length_y), :] = values[way]

    await_bytes(x_recv, x_send_sem)
    await_bytes(x_pair_recv, pair_send_sem)
    await_bytes(all_peers(y_matrix_recv, y_matrix_send), matrix_send_sem)
    await_bytes(all_peers(y_source_recv, y_source_send), source_send_sem)


def await_bytes(ref, sem):
    pltpu.make_async_copy(ref, ref, sem).wait()


def put_out(blocks_ref, out_hbm, sem):
    run = out_hbm.shape[0] // SUB
    stores = [
        pltpu.make_async_copy(
            blocks_ref.at[block, pl.ds((run + 1) * part, run)],
            out_hbm.at[pl.ds(run * part, run), pl.ds(LANES * block, LANES)],
            sem,
        )
        for block in range(blocks_ref.shape[0])
        for part in range(SUB)
    ]
    for store in stores:
        store.start()
    await_bytes(out_hbm, sem)


def body(initial_temp, kx_low, ky_low):
    count_x = lax.axis_size("gx")
    count_y = lax.axis_size("gy")
    _, rows, columns = initial_temp.shape
    length_x = columns // (WAYS * SUB)
    length_y = rows // (WAYS * SUB)
    blocks_x = rows // LANES
    blocks_y = columns // LANES

    def vmem(*shape):
        return pltpu.VMEM(shape, jnp.float32)

    def sems(*shape):
        return pltpu.SemaphoreType.DMA(shape)

    blocks = pl.pallas_call(
        functools.partial(kernel, count_x, count_y),
        out_shape=jax.ShapeDtypeStruct((blocks_y, rows + SUB, LANES), jnp.float32),
        in_specs=[pl.BlockSpec(memory_space=pltpu.HBM)] * 3,
        out_specs=pl.BlockSpec(memory_space=pltpu.VMEM),
        scratch_shapes=[
            vmem(rows, columns),
            vmem(rows, columns),
            vmem(rows, columns),
            vmem(blocks_y, rows + SUB, LANES),
            vmem(blocks_x, columns + SUB, LANES),
            vmem(blocks_x, columns + SUB, LANES),
            vmem(blocks_x, columns + SUB, LANES),
            vmem(blocks_y, rows + SUB, LANES),
            vmem(blocks_y, rows + SUB, LANES),
            vmem(blocks_y, rows + SUB, LANES),
            vmem(rows + SUB, LANES),
            vmem(rows + SUB, LANES),
            vmem(length_x - 1, WAYS, blocks_x, SUB, LANES),
            vmem(length_x - 1, WAYS, blocks_x, SUB, LANES),
            vmem(length_x - 1, WAYS, blocks_x, SUB, LANES),
            vmem(length_y - 1, WAYS, blocks_y, SUB, LANES),
            vmem(length_y - 1, WAYS, blocks_y, SUB, LANES),
            vmem(length_y - 1, WAYS, blocks_y, SUB, LANES),
            vmem(length_y - 1, WAYS, blocks_y, SUB, LANES),
            vmem(18, blocks_x, SUB, LANES),
            vmem(6, blocks_x, SUB, LANES),
            vmem(18, blocks_y, SUB, LANES),
            vmem(6, blocks_y, SUB, LANES),
            vmem(18, blocks_y, SUB, LANES),
            vmem(6, blocks_y, SUB, LANES),
            vmem(blocks_x, SUB, LANES),
            vmem(2, blocks_x, SUB, LANES),
            vmem(2 * REACH, blocks_x, SUB, LANES),
            vmem(2, blocks_x, SUB, LANES),
            vmem(blocks_y, 3, LANES),
            vmem(blocks_y, SUB * SLOT_RUN, LANES),
            vmem(blocks_y, 2, LANES),
            vmem(blocks_y, SUB * SLOT_RUN, LANES),
            sems(3),
        ]
        + [pltpu.SemaphoreType.DMA] * 8,
        compiler_params=pltpu.CompilerParams(
            collective_id=0, has_side_effects=True, vmem_limit_bytes=ROOM
        ),
    )(*(pltpu.with_memory_space_constraint(value[0], pltpu.HBM) for value in (initial_temp, kx_low, ky_low)))
    result = pl.pallas_call(
        put_out,
        out_shape=jax.ShapeDtypeStruct((rows, columns), jnp.float32),
        in_specs=[pl.BlockSpec(memory_space=pltpu.VMEM)],
        out_specs=pl.BlockSpec(memory_space=pltpu.HBM),
        scratch_shapes=[pltpu.SemaphoreType.DMA],
        compiler_params=pltpu.CompilerParams(vmem_limit_bytes=SMALL_ROOM),
    )(blocks)
    return result[None]


def solution(mesh):
    spec = P(None, "gy", "gx")
    return jax.shard_map(
        body, mesh=mesh, in_specs=(spec, spec, spec), out_specs=spec, check_vma=False
    )
```

```python
import functools

import jax
import jax.numpy as jnp
from jax import lax
from jax.experimental import pallas as pl
from jax.experimental.pallas import tpu as pltpu
from jax.sharding import PartitionSpec as P

MESH = pl.DeviceIdType.MESH
SUB = 8
LANES = 128
WAYS = 4
REACH = 4
SHORT = 1e30
RING = 4
SLOT_RUN = 36
ROOM = 24 * 1024 * 1024
SMALL_ROOM = 1024 * 1024


def recip(value):
    return pltpu.reciprocal(value, full_range=False)


def join_matrix(low, high):
    excess = low[1] + high[2]
    inverse = recip(excess + (low[0] + high[0]))
    to_low = low[0] * inverse
    to_high = high[0] * inverse
    joined = (to_low * high[0], high[1] + to_high * excess, low[2] + to_low * excess)
    return joined, (inverse, to_low, to_high)


def join_source(low, high, coefs):
    inverse, to_low, to_high = coefs
    source = low[0] + high[1]
    return (high[0] + to_high * source, low[1] + to_low * source), source * inverse


def next_rows(value, steps):
    return pltpu.roll(value, SUB - steps, 1)


def tree_matrix(blocks, coef_ref, lanes):
    def keep(slot, coefs):
        for place, coef in enumerate(coefs):
            coef_ref[3 * slot + place, lanes] = coef

    first, coefs = join_matrix(blocks[0], blocks[1])
    keep(0, coefs)
    second, coefs = join_matrix(blocks[2], blocks[3])
    keep(1, coefs)
    joined, coefs = join_matrix(first, second)
    keep(2, coefs)
    for level in range(3):
        other = tuple(next_rows(member, 1 << level) for member in joined)
        joined, coefs = join_matrix(joined, other)
        keep(3 + level, coefs)
    return joined


def tree_source(blocks, coef_ref, mid_ref, lanes):
    def coefs(slot):
        return tuple(coef_ref[3 * slot + place, lanes] for place in range(3))

    first, mid = join_source(blocks[0], blocks[1], coefs(0))
    mid_ref[0, lanes] = mid
    second, mid = join_source(blocks[2], blocks[3], coefs(1))
    mid_ref[1, lanes] = mid
    joined, mid = join_source(first, second, coefs(2))
    mid_ref[2, lanes] = mid
    for level in range(3):
        other = tuple(next_rows(member, 1 << level) for member in joined)
        joined, mid = join_source(joined, other, coefs(3 + level))
        mid_ref[3 + level, lanes] = mid
    return joined


def spread(value, level, row):
    for bit in range(level + 1):
        value = jnp.where((row & (1 << bit)) != 0, pltpu.roll(value, 1 << bit, 1), value)
    return value


def spread_coefs(coef_ref, lanes, row):
    for level in range(3):
        for place in (1, 2):
            slot = 3 * (3 + level) + place
            coef_ref[slot, lanes] = spread(coef_ref[slot, lanes], level, row)


def spread_mids(mid_ref, lanes, row):
    for level in range(3):
        mid_ref[3 + level, lanes] = spread(mid_ref[3 + level, lanes], level, row)


def tree_down(left, right, coef_ref, mid_ref, lanes, row):
    def middle(slot, low, high):
        value = coef_ref[3 * slot + 1, lanes] * low + coef_ref[3 * slot + 2, lanes] * high
        return value if mid_ref is None else mid_ref[slot, lanes] + value

    for level in (2, 1, 0):
        mid = middle(3 + level, left, right)
        lower = (row & (1 << level)) == 0
        left, right = jnp.where(lower, left, mid), jnp.where(lower, mid, right)
    center = middle(2, left, right)
    lower_mid = middle(0, left, center)
    upper_mid = middle(1, center, right)
    return (left, lower_mid, center, upper_mid, right)


def solve_pair(own_matrix, own_source, rest_matrix, rest_source):
    link = own_matrix[0] + rest_matrix[0]
    own_excess = own_matrix[1] + rest_matrix[2]
    prev_excess = own_matrix[2] + rest_matrix[1]
    own_total = own_source[0] + rest_source[1]
    prev_total = own_source[1] + rest_source[0]
    inverse = recip(own_excess * prev_excess + link * (own_excess + prev_excess))
    both = link * (own_total + prev_total)
    own_value = (own_total * prev_excess + both) * inverse
    prev_value = (prev_total * own_excess + both) * inverse
    return own_value, prev_value


def kernel(
    count_x,
    count_y,
    temp_hbm,
    kx_hbm,
    ky_hbm,
    out_ref,
    temp_ref,
    kx_ref,
    ky_flat,
    ky_ref,
    temp_turned,
    kx_turned,
    third_turned,
    local_field,
    left_field,
    right_field,
    own_column,
    prev_column,
    x_link,
    x_next,
    x_mid,
    y_link,
    y_next,
    y_inverse,
    y_mid,
    x_coefs,
    x_mids,
    y_coefs,
    y_mids,
    ring_coefs,
    ring_mids,
    x_send,
    x_pair_send,
    x_recv,
    x_pair_recv,
    y_matrix_send,
    y_matrix_recv,
    y_source_send,
    y_source_recv,
    in_sems,
    x_send_sem,
    x_recv_sem,
    pair_send_sem,
    pair_recv_sem,
    matrix_send_sem,
    matrix_recv_sem,
    source_send_sem,
    source_recv_sem,
    rings_sem,
    partner_sem,
):
    rows, columns = temp_ref.shape
    blocks_x = rows // LANES
    blocks_y = columns // LANES
    my_x = lax.axis_index("gx")
    my_y = lax.axis_index("gy")
    loads = [
        pltpu.make_async_copy(kx_hbm, kx_ref, in_sems.at[0]),
        pltpu.make_async_copy(temp_hbm, temp_ref, in_sems.at[1]),
        pltpu.make_async_copy(ky_hbm, ky_flat, in_sems.at[2]),
    ]
    for load in loads:
        load.start()

    def peer_x(offset):
        return {"gx": lax.rem(my_x + (offset + count_x), count_x)}

    def peer_y(offset):
        return {"gy": lax.rem(my_y + offset, count_y)}

    offsets = [sign * step for step in range(REACH, 0, -1) for sign in (1, -1)]

    def hops_y(offset):
        ring = offset // 2 // RING % RING
        place = offset // 2 % RING
        return min(ring, RING - ring) + min(place, RING - place)

    offsets_y = sorted(range(1, count_y), key=lambda offset: -hops_y(offset))
    barrier = pltpu.get_barrier_semaphore()
    for offset in offsets:
        pl.semaphore_signal(barrier, inc=1, device_id=peer_x(offset), device_id_type=MESH)

    core = lax.rem(my_y, 2)
    place = lax.rem(my_y // 2, RING)
    ring = my_y // (2 * RING)

    def at(ring, place, core):
        return {"gy": (ring * RING + place) * 2 + core}

    own_ring = [at(ring, lax.rem(place + step, RING), core) for step in (2, 1, 3)]
    other_rings = [at(lax.rem(ring + step, RING), place, core) for step in (2, 1, 3)]
    partner = at(ring, place, 1 - core)
    for peer in own_ring + other_rings + [partner]:
        pl.semaphore_signal(barrier, inc=1, device_id=peer, device_id_type=MESH)

    def slot_of(offset):
        return offset + REACH - (1 if offset > 0 else 0)

    shape_x = (blocks_x, SUB, LANES)
    row_x = lax.broadcasted_iota(jnp.int32, shape_x, 1)
    every = slice(0, blocks_x)
    length_x = columns // (WAYS * SUB)
    length_y = rows // (WAYS * SUB)

    def rows_of(way, step, length):
        return pl.ds(way * length + step, SUB, stride=WAYS * length + 1)

    def put(target, first, values, length):
        run = WAYS * length
        for top in range(0, values.shape[0], min(run, values.shape[0])):
            place = first + top
            target[pl.ds(place + place // run, min(run, values.shape[0])), :] = values[
                top : top + min(run, values.shape[0])
            ]

    def turn_in(source, target):
        for block in range(blocks_x):
            for left in range(0, columns, LANES):
                put(
                    target.at[block],
                    left,
                    source[LANES * block : LANES * (block + 1), left : left + LANES].T,
                    length_x,
                )

    loads[0].wait()
    turn_in(kx_ref, kx_turned)
    loads[1].wait()
    turn_in(temp_ref, temp_turned)

    excess = [jnp.ones(shape_x, jnp.float32)] * WAYS
    link = [kx_turned[:, rows_of(way, 0, length_x), :] for way in range(WAYS)]
    source = [temp_turned[:, rows_of(way, 0, length_x), :] for way in range(WAYS)]
    left_excess = [jnp.zeros(shape_x, jnp.float32)] * WAYS
    left_source = [jnp.zeros(shape_x, jnp.float32)] * WAYS
    for step in range(length_x - 1):
        for way in range(WAYS):
            face = kx_turned[:, rows_of(way, step + 1, length_x), :]
            inverse = recip(excess[way] + link[way] + face)
            to_next = face * inverse
            to_left = link[way] * inverse
            x_next[step, way] = to_next
            x_link[step, way] = to_left
            x_mid[step, way] = source[way] * inverse
            left_excess[way] = left_excess[way] + to_left * excess[way]
            left_source[way] = left_source[way] + to_left * source[way]
            link[way] = to_left * face
            excess[way] = 1.0 + to_next * excess[way]
            source[way] = (
                temp_turned[:, rows_of(way, step + 1, length_x), :] + to_next * source[way]
            )
    matrix = [(link[way], excess[way], left_excess[way]) for way in range(WAYS)]
    own_matrix = tree_matrix(matrix, x_coefs, every)
    own_source = tree_source(
        [(source[way], left_source[way]) for way in range(WAYS)], x_coefs, x_mids, every
    )
    for place, member in enumerate(own_matrix + own_source):
        x_send[:, place : place + 1, :] = member[:, 0:1, :]

    pl.semaphore_wait(barrier, len(offsets) + len(own_ring) + len(other_rings) + 1)

    for offset in offsets:
        pltpu.make_async_remote_copy(
            src_ref=x_send,
            dst_ref=x_recv.at[slot_of(-offset)],
            send_sem=x_send_sem,
            recv_sem=x_recv_sem,
            device_id=peer_x(offset),
            device_id_type=MESH,
        ).start()

    for peer in other_rings:
        pl.semaphore_signal(rings_sem, inc=1, device_id=peer, device_id_type=MESH)

    loads[2].wait()
    for block in range(blocks_y):
        put(ky_ref.at[block], 0, ky_flat[:, LANES * block : LANES * (block + 1)], length_y)
    width = 2
    shape_y = (width, SUB, LANES)
    groups = [slice(start, start + width) for start in range(0, blocks_y, width)]
    row_y = lax.broadcasted_iota(jnp.int32, shape_y, 1)
    for lanes in groups:
        excess = [jnp.ones(shape_y, jnp.float32)] * WAYS
        link = [ky_ref[lanes, rows_of(way, 0, length_y), :] for way in range(WAYS)]
        left_excess = [jnp.zeros(shape_y, jnp.float32)] * WAYS
        for step in range(length_y - 1):
            for way in range(WAYS):
                face = ky_ref[lanes, rows_of(way, step + 1, length_y), :]
                inverse = recip(excess[way] + link[way] + face)
                to_next = face * inverse
                to_left = link[way] * inverse
                y_next[step, way, lanes] = to_next
                y_link[step, way, lanes] = to_left
                y_inverse[step, way, lanes] = inverse
                left_excess[way] = left_excess[way] + to_left * excess[way]
                link[way] = to_left * face
                excess[way] = 1.0 + to_next * excess[way]
        matrix = [(link[way], excess[way], left_excess[way]) for way in range(WAYS)]
        joined = tree_matrix(matrix, y_coefs, lanes)
        for place, member in enumerate(joined):
            y_matrix_send[lanes, place : place + 1, :] = member[:, 0:1, :]

    def row_of_slot(slot):
        return SLOT_RUN * (slot // WAYS) + SUB * (slot % WAYS)

    def to_y_peers(source, target, send_sem, recv_sem):
        height = source.shape[1]
        for offset in offsets_y:
            slot = count_y - 1 - offset
            pltpu.make_async_remote_copy(
                src_ref=source,
                dst_ref=target.at[:, pl.ds(row_of_slot(slot), height), :],
                send_sem=send_sem,
                recv_sem=recv_sem,
                device_id=peer_y(offset),
                device_id_type=MESH,
            ).start()

    def all_peers(target, source):
        return target.at[:, pl.ds(0, source.shape[1] * (count_y - 1)), :]


    spare = row_of_slot(count_y - 1)
    y_matrix_recv[:, spare : spare + 1, :] = jnp.full((blocks_y, 1, LANES), SHORT, jnp.float32)
    y_matrix_recv[:, spare + 1 : spare + 3, :] = jnp.zeros((blocks_y, 2, LANES), jnp.float32)
    y_source_recv[:, spare : spare + 2, :] = jnp.zeros((blocks_y, 2, LANES), jnp.float32)
    spread_coefs(x_coefs, every, row_x)
    spread_mids(x_mids, every, row_x)

    zeros = jnp.zeros(shape_x, jnp.float32)
    ones = jnp.ones(shape_x, jnp.float32)
    for left, right, mids, cells, turned, field in (
        (zeros, zeros, x_mids, x_mid, temp_turned, local_field),
        (ones, zeros, None, None, kx_turned, left_field),
        (zeros, ones, None, None, third_turned, right_field),
    ):
        nodes = tree_down(left, right, x_coefs, mids, every, row_x)
        values = list(nodes[1:])
        for way in range(WAYS):
            turned[:, rows_of(way, length_x - 1, length_x), :] = values[way]
        for step in range(length_x - 2, -1, -1):
            for way in range(WAYS):
                value = x_link[step, way] * nodes[way] + x_next[step, way] * values[way]
                values[way] = value if cells is None else cells[step, way] + value
                turned[:, rows_of(way, step, length_x), :] = values[way]
        for block in range(blocks_x):
            for other in range(blocks_y):
                run = WAYS * length_x
                parts = [
                    turned[block, pl.ds(place + place // run, run), :]
                    for place in range(LANES * other, LANES * (other + 1), run)
                ]
                put(field.at[other], LANES * block, jnp.concatenate(parts, axis=0).T, length_y)

    def load_block(ref):
        return (
            tuple(ref[:, place : place + 1, :] for place in range(3)),
            tuple(ref[:, place : place + 1, :] for place in range(3, 5)),
        )

    def join(low, high):
        matrix, coefs = join_matrix(low[0], high[0])
        source, _ = join_source(low[1], high[1], coefs)
        return matrix, source

    await_bytes(x_recv, x_recv_sem)
    near = {offset: load_block(x_recv.at[slot_of(offset)]) for offset in offsets}
    above = join(join(near[1], near[2]), join(near[3], near[4]))
    below_three = join(near[-3], join(near[-2], near[-1]))
    below = join(near[-4], below_three)
    for place, (block, offset) in enumerate(((above, -REACH), (below_three, REACH))):
        for index, member in enumerate(block[0] + block[1]):
            x_pair_send[place, :, index : index + 1, :] = member
        pltpu.make_async_remote_copy(
            src_ref=x_pair_send.at[place],
            dst_ref=x_pair_recv.at[place],
            send_sem=pair_send_sem,
            recv_sem=pair_recv_sem,
            device_id=peer_x(offset),
            device_id_type=MESH,
        ).start()

    pl.semaphore_wait(rings_sem, len(other_rings))
    pl.semaphore_signal(partner_sem, inc=1, device_id=partner, device_id_type=MESH)
    pl.semaphore_wait(partner_sem, 1)
    to_y_peers(y_matrix_send, y_matrix_recv, matrix_send_sem, matrix_recv_sem)

    await_bytes(x_pair_recv, pair_recv_sem)
    far_above = load_block(x_pair_recv.at[0])
    far_below = load_block(x_pair_recv.at[1])
    rest = join(join(above, far_above), join(far_below, below))
    own = load_block(x_send)
    own_value, prev_value = solve_pair(own[0], own[1], rest[0], rest[1])

    for value, column in ((own_value, own_column), (prev_value, prev_column)):
        for block in range(blocks_x):
            put(column, LANES * block, jnp.broadcast_to(value[block], (LANES, LANES)).T, length_y)

    def half_rows(lanes, way, step):
        rows_here = rows_of(way, step, length_y)
        return (
            local_field[lanes, rows_here, :]
            + prev_column[rows_here, :] * left_field[lanes, rows_here, :]
            + own_column[rows_here, :] * right_field[lanes, rows_here, :]
        )

    for lanes in groups:
        source = [half_rows(lanes, way, 0) for way in range(WAYS)]
        left_source = [jnp.zeros(shape_y, jnp.float32)] * WAYS
        for step in range(length_y - 1):
            for way in range(WAYS):
                y_mid[step, way, lanes] = source[way] * y_inverse[step, way, lanes]
                left_source[way] = left_source[way] + y_link[step, way, lanes] * source[way]
                source[way] = (
                    half_rows(lanes, way, step + 1)
                    + y_next[step, way, lanes] * source[way]
                )
        joined = tree_source(
            [(source[way], left_source[way]) for way in range(WAYS)], y_coefs, y_mids, lanes
        )
        for place, member in enumerate(joined):
            y_source_send[lanes, place : place + 1, :] = member[:, 0:1, :]
    to_y_peers(y_source_send, y_source_recv, source_send_sem, source_recv_sem)
    for lanes in groups:
        spread_coefs(y_coefs, lanes, row_y)
        spread_mids(y_mids, lanes, row_y)
    await_bytes(all_peers(y_matrix_recv, y_matrix_send), matrix_recv_sem)
    rings = []
    for lanes in groups:
        blocks = [
            tuple(
                y_matrix_recv[lanes, pl.ds(SUB * way + place, SUB, stride=SLOT_RUN), :]
                for place in range(3)
            )
            for way in range(WAYS)
        ]
        rings.append(tree_matrix(blocks, ring_coefs, lanes))

    await_bytes(all_peers(y_source_recv, y_source_send), source_recv_sem)

    for group, lanes in enumerate(groups):
        blocks = [
            tuple(
                y_source_recv[lanes, pl.ds(SUB * way + place, SUB, stride=SLOT_RUN), :]
                for place in range(2)
            )
            for way in range(WAYS)
        ]
        ring_source = tree_source(blocks, ring_coefs, ring_mids, lanes)
        own_value, prev_value = solve_pair(
            tuple(y_matrix_send[lanes, place : place + 1, :] for place in range(3)),
            tuple(y_source_send[lanes, place : place + 1, :] for place in range(2)),
            tuple(member[:, 0:1, :] for member in rings[group]),
            tuple(member[:, 0:1, :] for member in ring_source),
        )
        nodes = tree_down(
            jnp.broadcast_to(prev_value, shape_y),
            jnp.broadcast_to(own_value, shape_y),
            y_coefs,
            y_mids,
            lanes,
            row_y,
        )
        values = list(nodes[1:])
        for way in range(WAYS):
            out_ref[lanes, rows_of(way, length_y - 1, length_y), :] = values[way]
        for step in range(length_y - 2, -1, -1):
            for way in range(WAYS):
                values[way] = (
                    y_mid[step, way, lanes] + y_link[step, way, lanes] * nodes[way]
                ) + y_next[step, way, lanes] * values[way]
                out_ref[lanes, rows_of(way, step, length_y), :] = values[way]

    await_bytes(x_recv, x_send_sem)
    await_bytes(x_pair_recv, pair_send_sem)
    await_bytes(all_peers(y_matrix_recv, y_matrix_send), matrix_send_sem)
    await_bytes(all_peers(y_source_recv, y_source_send), source_send_sem)


def await_bytes(ref, sem):
    pltpu.make_async_copy(ref, ref, sem).wait()


def put_out(blocks_ref, out_hbm, sem):
    run = out_hbm.shape[0] // SUB
    stores = [
        pltpu.make_async_copy(
            blocks_ref.at[block, pl.ds((run + 1) * part, run)],
            out_hbm.at[pl.ds(run * part, run), pl.ds(LANES * block, LANES)],
            sem,
        )
        for block in range(blocks_ref.shape[0])
        for part in range(SUB)
    ]
    for store in stores:
        store.start()
    await_bytes(out_hbm, sem)


def body(initial_temp, kx_low, ky_low):
    count_x = lax.axis_size("gx")
    count_y = lax.axis_size("gy")
    _, rows, columns = initial_temp.shape
    length_x = columns // (WAYS * SUB)
    length_y = rows // (WAYS * SUB)
    blocks_x = rows // LANES
    blocks_y = columns // LANES

    def vmem(*shape):
        return pltpu.VMEM(shape, jnp.float32)

    def sems(*shape):
        return pltpu.SemaphoreType.DMA(shape)

    blocks = pl.pallas_call(
        functools.partial(kernel, count_x, count_y),
        out_shape=jax.ShapeDtypeStruct((blocks_y, rows + SUB, LANES), jnp.float32),
        in_specs=[pl.BlockSpec(memory_space=pltpu.HBM)] * 3,
        out_specs=pl.BlockSpec(memory_space=pltpu.VMEM),
        scratch_shapes=[
            vmem(rows, columns),
            vmem(rows, columns),
            vmem(rows, columns),
            vmem(blocks_y, rows + SUB, LANES),
            vmem(blocks_x, columns + SUB, LANES),
            vmem(blocks_x, columns + SUB, LANES),
            vmem(blocks_x, columns + SUB, LANES),
            vmem(blocks_y, rows + SUB, LANES),
            vmem(blocks_y, rows + SUB, LANES),
            vmem(blocks_y, rows + SUB, LANES),
            vmem(rows + SUB, LANES),
            vmem(rows + SUB, LANES),
            vmem(length_x - 1, WAYS, blocks_x, SUB, LANES),
            vmem(length_x - 1, WAYS, blocks_x, SUB, LANES),
            vmem(length_x - 1, WAYS, blocks_x, SUB, LANES),
            vmem(length_y - 1, WAYS, blocks_y, SUB, LANES),
            vmem(length_y - 1, WAYS, blocks_y, SUB, LANES),
            vmem(length_y - 1, WAYS, blocks_y, SUB, LANES),
            vmem(length_y - 1, WAYS, blocks_y, SUB, LANES),
            vmem(18, blocks_x, SUB, LANES),
            vmem(6, blocks_x, SUB, LANES),
            vmem(18, blocks_y, SUB, LANES),
            vmem(6, blocks_y, SUB, LANES),
            vmem(18, blocks_y, SUB, LANES),
            vmem(6, blocks_y, SUB, LANES),
            vmem(blocks_x, SUB, LANES),
            vmem(2, blocks_x, SUB, LANES),
            vmem(2 * REACH, blocks_x, SUB, LANES),
            vmem(2, blocks_x, SUB, LANES),
            vmem(blocks_y, 3, LANES),
            vmem(blocks_y, SUB * SLOT_RUN, LANES),
            vmem(blocks_y, 2, LANES),
            vmem(blocks_y, SUB * SLOT_RUN, LANES),
            sems(3),
        ]
        + [pltpu.SemaphoreType.DMA] * 8
        + [pltpu.SemaphoreType.REGULAR] * 2,
        compiler_params=pltpu.CompilerParams(
            collective_id=0, has_side_effects=True, vmem_limit_bytes=ROOM
        ),
    )(*(pltpu.with_memory_space_constraint(value[0], pltpu.HBM) for value in (initial_temp, kx_low, ky_low)))
    result = pl.pallas_call(
        put_out,
        out_shape=jax.ShapeDtypeStruct((rows, columns), jnp.float32),
        in_specs=[pl.BlockSpec(memory_space=pltpu.VMEM)],
        out_specs=pl.BlockSpec(memory_space=pltpu.HBM),
        scratch_shapes=[pltpu.SemaphoreType.DMA],
        compiler_params=pltpu.CompilerParams(vmem_limit_bytes=SMALL_ROOM),
    )(blocks)
    return result[None]


def solution(mesh):
    spec = P(None, "gy", "gx")
    return jax.shard_map(
        body, mesh=mesh, in_specs=(spec, spec, spec), out_specs=spec, check_vma=False
    )
```

```python
import functools

import jax
import jax.numpy as jnp
from jax import lax
from jax.experimental import pallas as pl
from jax.experimental.pallas import tpu as pltpu
from jax.sharding import PartitionSpec as P

MESH = pl.DeviceIdType.MESH
SUB = 8
LANES = 128
WAYS = 4
REACH = 4
SHORT = 1e30
RING = 4
SLOT_RUN = 36
ROOM = 24 * 1024 * 1024
SMALL_ROOM = 1024 * 1024


def recip(value):
    return pltpu.reciprocal(value, full_range=False)


def join_matrix(low, high):
    excess = low[1] + high[2]
    inverse = recip(excess + (low[0] + high[0]))
    to_low = low[0] * inverse
    to_high = high[0] * inverse
    joined = (to_low * high[0], high[1] + to_high * excess, low[2] + to_low * excess)
    return joined, (inverse, to_low, to_high)


def join_source(low, high, coefs):
    inverse, to_low, to_high = coefs
    source = low[0] + high[1]
    return (high[0] + to_high * source, low[1] + to_low * source), source * inverse


def next_rows(value, steps):
    return pltpu.roll(value, SUB - steps, 1)


def tree_matrix(blocks, coef_ref, lanes):
    def keep(slot, coefs):
        for place, coef in enumerate(coefs):
            coef_ref[3 * slot + place, lanes] = coef

    first, coefs = join_matrix(blocks[0], blocks[1])
    keep(0, coefs)
    second, coefs = join_matrix(blocks[2], blocks[3])
    keep(1, coefs)
    joined, coefs = join_matrix(first, second)
    keep(2, coefs)
    for level in range(3):
        other = tuple(next_rows(member, 1 << level) for member in joined)
        joined, coefs = join_matrix(joined, other)
        keep(3 + level, coefs)
    return joined


def tree_source(blocks, coef_ref, mid_ref, lanes):
    def coefs(slot):
        return tuple(coef_ref[3 * slot + place, lanes] for place in range(3))

    first, mid = join_source(blocks[0], blocks[1], coefs(0))
    mid_ref[0, lanes] = mid
    second, mid = join_source(blocks[2], blocks[3], coefs(1))
    mid_ref[1, lanes] = mid
    joined, mid = join_source(first, second, coefs(2))
    mid_ref[2, lanes] = mid
    for level in range(3):
        other = tuple(next_rows(member, 1 << level) for member in joined)
        joined, mid = join_source(joined, other, coefs(3 + level))
        mid_ref[3 + level, lanes] = mid
    return joined


def spread(value, level, row):
    for bit in range(level + 1):
        value = jnp.where((row & (1 << bit)) != 0, pltpu.roll(value, 1 << bit, 1), value)
    return value


def spread_coefs(coef_ref, lanes, row):
    for level in range(3):
        for place in (1, 2):
            slot = 3 * (3 + level) + place
            coef_ref[slot, lanes] = spread(coef_ref[slot, lanes], level, row)


def spread_mids(mid_ref, lanes, row):
    for level in range(3):
        mid_ref[3 + level, lanes] = spread(mid_ref[3 + level, lanes], level, row)


def tree_down(left, right, coef_ref, mid_ref, lanes, row):
    def middle(slot, low, high):
        value = coef_ref[3 * slot + 1, lanes] * low + coef_ref[3 * slot + 2, lanes] * high
        return value if mid_ref is None else mid_ref[slot, lanes] + value

    for level in (2, 1, 0):
        mid = middle(3 + level, left, right)
        lower = (row & (1 << level)) == 0
        left, right = jnp.where(lower, left, mid), jnp.where(lower, mid, right)
    center = middle(2, left, right)
    lower_mid = middle(0, left, center)
    upper_mid = middle(1, center, right)
    return (left, lower_mid, center, upper_mid, right)


def solve_pair(own_matrix, own_source, rest_matrix, rest_source):
    link = own_matrix[0] + rest_matrix[0]
    own_excess = own_matrix[1] + rest_matrix[2]
    prev_excess = own_matrix[2] + rest_matrix[1]
    own_total = own_source[0] + rest_source[1]
    prev_total = own_source[1] + rest_source[0]
    inverse = recip(own_excess * prev_excess + link * (own_excess + prev_excess))
    both = link * (own_total + prev_total)
    own_value = (own_total * prev_excess + both) * inverse
    prev_value = (prev_total * own_excess + both) * inverse
    return own_value, prev_value


def kernel(
    count_x,
    count_y,
    temp_hbm,
    kx_hbm,
    ky_hbm,
    out_ref,
    temp_ref,
    kx_ref,
    ky_flat,
    ky_ref,
    temp_turned,
    kx_turned,
    third_turned,
    local_field,
    left_field,
    right_field,
    own_column,
    prev_column,
    x_link,
    x_next,
    x_mid,
    y_link,
    y_next,
    y_inverse,
    y_mid,
    x_coefs,
    x_mids,
    y_coefs,
    y_mids,
    ring_coefs,
    ring_mids,
    x_send,
    x_pair_send,
    x_recv,
    x_pair_recv,
    y_matrix_send,
    y_matrix_recv,
    y_source_send,
    y_source_recv,
    in_sems,
    x_send_sem,
    x_recv_sems,
    pair_send_sem,
    pair_recv_sem,
    matrix_send_sem,
    matrix_recv_sem,
    source_send_sem,
    source_recv_sem,
    rings_sem,
    partner_sem,
):
    rows, columns = temp_ref.shape
    blocks_x = rows // LANES
    blocks_y = columns // LANES
    my_x = lax.axis_index("gx")
    my_y = lax.axis_index("gy")
    loads = [
        pltpu.make_async_copy(kx_hbm, kx_ref, in_sems.at[0]),
        pltpu.make_async_copy(temp_hbm, temp_ref, in_sems.at[1]),
        pltpu.make_async_copy(ky_hbm, ky_flat, in_sems.at[2]),
    ]
    for load in loads:
        load.start()

    def peer_x(offset):
        return {"gx": lax.rem(my_x + (offset + count_x), count_x)}

    def peer_y(offset):
        return {"gy": lax.rem(my_y + offset, count_y)}

    offsets = [sign * step for step in range(REACH, 0, -1) for sign in (1, -1)]

    def hops_y(offset):
        ring = offset // 2 // RING % RING
        place = offset // 2 % RING
        return min(ring, RING - ring) + min(place, RING - place)

    offsets_y = sorted(range(1, count_y), key=lambda offset: -hops_y(offset))
    barrier = pltpu.get_barrier_semaphore()
    for offset in offsets:
        pl.semaphore_signal(barrier, inc=1, device_id=peer_x(offset), device_id_type=MESH)

    core = lax.rem(my_y, 2)
    place = lax.rem(my_y // 2, RING)
    ring = my_y // (2 * RING)

    def at(ring, place, core):
        return {"gy": (ring * RING + place) * 2 + core}

    own_ring = [at(ring, lax.rem(place + step, RING), core) for step in (2, 1, 3)]
    other_rings = [at(lax.rem(ring + step, RING), place, core) for step in (2, 1, 3)]
    partner = at(ring, place, 1 - core)
    for peer in own_ring + other_rings + [partner]:
        pl.semaphore_signal(barrier, inc=1, device_id=peer, device_id_type=MESH)

    def slot_of(offset):
        return offset + REACH - (1 if offset > 0 else 0)

    shape_x = (blocks_x, SUB, LANES)
    row_x = lax.broadcasted_iota(jnp.int32, shape_x, 1)
    every = slice(0, blocks_x)
    length_x = columns // (WAYS * SUB)
    length_y = rows // (WAYS * SUB)

    def rows_of(way, step, length):
        return pl.ds(way * length + step, SUB, stride=WAYS * length + 1)

    def put(target, first, values, length):
        run = WAYS * length
        for top in range(0, values.shape[0], min(run, values.shape[0])):
            place = first + top
            target[pl.ds(place + place // run, min(run, values.shape[0])), :] = values[
                top : top + min(run, values.shape[0])
            ]

    def turn_in(source, target):
        for block in range(blocks_x):
            for left in range(0, columns, LANES):
                put(
                    target.at[block],
                    left,
                    source[LANES * block : LANES * (block + 1), left : left + LANES].T,
                    length_x,
                )

    loads[0].wait()
    turn_in(kx_ref, kx_turned)
    loads[1].wait()
    turn_in(temp_ref, temp_turned)

    excess = [jnp.ones(shape_x, jnp.float32)] * WAYS
    link = [kx_turned[:, rows_of(way, 0, length_x), :] for way in range(WAYS)]
    source = [temp_turned[:, rows_of(way, 0, length_x), :] for way in range(WAYS)]
    left_excess = [jnp.zeros(shape_x, jnp.float32)] * WAYS
    left_source = [jnp.zeros(shape_x, jnp.float32)] * WAYS
    for step in range(length_x - 1):
        for way in range(WAYS):
            face = kx_turned[:, rows_of(way, step + 1, length_x), :]
            inverse = recip(excess[way] + link[way] + face)
            to_next = face * inverse
            to_left = link[way] * inverse
            x_next[step, way] = to_next
            x_link[step, way] = to_left
            x_mid[step, way] = source[way] * inverse
            left_excess[way] = left_excess[way] + to_left * excess[way]
            left_source[way] = left_source[way] + to_left * source[way]
            link[way] = to_left * face
            excess[way] = 1.0 + to_next * excess[way]
            source[way] = (
                temp_turned[:, rows_of(way, step + 1, length_x), :] + to_next * source[way]
            )
    matrix = [(link[way], excess[way], left_excess[way]) for way in range(WAYS)]
    own_matrix = tree_matrix(matrix, x_coefs, every)
    own_source = tree_source(
        [(source[way], left_source[way]) for way in range(WAYS)], x_coefs, x_mids, every
    )
    for place, member in enumerate(own_matrix + own_source):
        x_send[:, place : place + 1, :] = member[:, 0:1, :]

    pl.semaphore_wait(barrier, len(offsets) + len(own_ring) + len(other_rings) + 1)

    for offset in offsets:
        pltpu.make_async_remote_copy(
            src_ref=x_send,
            dst_ref=x_recv.at[slot_of(-offset)],
            send_sem=x_send_sem,
            recv_sem=x_recv_sems.at[1 if offset < 0 else 0],
            device_id=peer_x(offset),
            device_id_type=MESH,
        ).start()

    for peer in other_rings:
        pl.semaphore_signal(rings_sem, inc=1, device_id=peer, device_id_type=MESH)

    loads[2].wait()
    for block in range(blocks_y):
        put(ky_ref.at[block], 0, ky_flat[:, LANES * block : LANES * (block + 1)], length_y)
    width = 2
    shape_y = (width, SUB, LANES)
    groups = [slice(start, start + width) for start in range(0, blocks_y, width)]
    row_y = lax.broadcasted_iota(jnp.int32, shape_y, 1)
    for lanes in groups:
        excess = [jnp.ones(shape_y, jnp.float32)] * WAYS
        link = [ky_ref[lanes, rows_of(way, 0, length_y), :] for way in range(WAYS)]
        left_excess = [jnp.zeros(shape_y, jnp.float32)] * WAYS
        for step in range(length_y - 1):
            for way in range(WAYS):
                face = ky_ref[lanes, rows_of(way, step + 1, length_y), :]
                inverse = recip(excess[way] + link[way] + face)
                to_next = face * inverse
                to_left = link[way] * inverse
                y_next[step, way, lanes] = to_next
                y_link[step, way, lanes] = to_left
                y_inverse[step, way, lanes] = inverse
                left_excess[way] = left_excess[way] + to_left * excess[way]
                link[way] = to_left * face
                excess[way] = 1.0 + to_next * excess[way]
        matrix = [(link[way], excess[way], left_excess[way]) for way in range(WAYS)]
        joined = tree_matrix(matrix, y_coefs, lanes)
        for place, member in enumerate(joined):
            y_matrix_send[lanes, place : place + 1, :] = member[:, 0:1, :]

    def row_of_slot(slot):
        return SLOT_RUN * (slot // WAYS) + SUB * (slot % WAYS)

    def to_y_peers(source, target, send_sem, recv_sem):
        height = source.shape[1]
        for offset in offsets_y:
            slot = count_y - 1 - offset
            pltpu.make_async_remote_copy(
                src_ref=source,
                dst_ref=target.at[:, pl.ds(row_of_slot(slot), height), :],
                send_sem=send_sem,
                recv_sem=recv_sem,
                device_id=peer_y(offset),
                device_id_type=MESH,
            ).start()

    def all_peers(target, source):
        return target.at[:, pl.ds(0, source.shape[1] * (count_y - 1)), :]


    spare = row_of_slot(count_y - 1)
    y_matrix_recv[:, spare : spare + 1, :] = jnp.full((blocks_y, 1, LANES), SHORT, jnp.float32)
    y_matrix_recv[:, spare + 1 : spare + 3, :] = jnp.zeros((blocks_y, 2, LANES), jnp.float32)
    y_source_recv[:, spare : spare + 2, :] = jnp.zeros((blocks_y, 2, LANES), jnp.float32)
    spread_coefs(x_coefs, every, row_x)
    spread_mids(x_mids, every, row_x)

    zeros = jnp.zeros(shape_x, jnp.float32)
    ones = jnp.ones(shape_x, jnp.float32)
    for left, right, mids, cells, turned, field in (
        (zeros, zeros, x_mids, x_mid, temp_turned, local_field),
        (ones, zeros, None, None, kx_turned, left_field),
        (zeros, ones, None, None, third_turned, right_field),
    ):
        nodes = tree_down(left, right, x_coefs, mids, every, row_x)
        values = list(nodes[1:])
        for way in range(WAYS):
            turned[:, rows_of(way, length_x - 1, length_x), :] = values[way]
        for step in range(length_x - 2, -1, -1):
            for way in range(WAYS):
                value = x_link[step, way] * nodes[way] + x_next[step, way] * values[way]
                values[way] = value if cells is None else cells[step, way] + value
                turned[:, rows_of(way, step, length_x), :] = values[way]
        for block in range(blocks_x):
            for other in range(blocks_y):
                run = WAYS * length_x
                parts = [
                    turned[block, pl.ds(place + place // run, run), :]
                    for place in range(LANES * other, LANES * (other + 1), run)
                ]
                put(field.at[other], LANES * block, jnp.concatenate(parts, axis=0).T, length_y)

    def load_block(ref):
        return (
            tuple(ref[:, place : place + 1, :] for place in range(3)),
            tuple(ref[:, place : place + 1, :] for place in range(3, 5)),
        )

    def join(low, high):
        matrix, coefs = join_matrix(low[0], high[0])
        source, _ = join_source(low[1], high[1], coefs)
        return matrix, source

    def near(offset):
        return load_block(x_recv.at[slot_of(offset)])

    for place, offset in ((0, -REACH), (1, REACH)):
        side = 1 - place
        await_bytes(x_recv.at[pl.ds(REACH * side, REACH)], x_recv_sems.at[side])
        if side == 1:
            above = join(join(near(1), near(2)), join(near(3), near(4)))
            block = above
        else:
            below_three = join(near(-3), join(near(-2), near(-1)))
            block = below_three
        for index, member in enumerate(block[0] + block[1]):
            x_pair_send[place, :, index : index + 1, :] = member
        pltpu.make_async_remote_copy(
            src_ref=x_pair_send.at[place],
            dst_ref=x_pair_recv.at[place],
            send_sem=pair_send_sem,
            recv_sem=pair_recv_sem,
            device_id=peer_x(offset),
            device_id_type=MESH,
        ).start()

    below = join(near(-4), below_three)

    pl.semaphore_wait(rings_sem, len(other_rings))
    pl.semaphore_signal(partner_sem, inc=1, device_id=partner, device_id_type=MESH)
    pl.semaphore_wait(partner_sem, 1)
    to_y_peers(y_matrix_send, y_matrix_recv, matrix_send_sem, matrix_recv_sem)

    await_bytes(x_pair_recv, pair_recv_sem)
    far_above = load_block(x_pair_recv.at[0])
    far_below = load_block(x_pair_recv.at[1])
    rest = join(join(above, far_above), join(far_below, below))
    own = load_block(x_send)
    own_value, prev_value = solve_pair(own[0], own[1], rest[0], rest[1])

    for value, column in ((own_value, own_column), (prev_value, prev_column)):
        for block in range(blocks_x):
            put(column, LANES * block, jnp.broadcast_to(value[block], (LANES, LANES)).T, length_y)

    def half_rows(lanes, way, step):
        rows_here = rows_of(way, step, length_y)
        return (
            local_field[lanes, rows_here, :]
            + prev_column[rows_here, :] * left_field[lanes, rows_here, :]
            + own_column[rows_here, :] * right_field[lanes, rows_here, :]
        )

    for lanes in groups:
        source = [half_rows(lanes, way, 0) for way in range(WAYS)]
        left_source = [jnp.zeros(shape_y, jnp.float32)] * WAYS
        for step in range(length_y - 1):
            for way in range(WAYS):
                y_mid[step, way, lanes] = source[way] * y_inverse[step, way, lanes]
                left_source[way] = left_source[way] + y_link[step, way, lanes] * source[way]
                source[way] = (
                    half_rows(lanes, way, step + 1)
                    + y_next[step, way, lanes] * source[way]
                )
        joined = tree_source(
            [(source[way], left_source[way]) for way in range(WAYS)], y_coefs, y_mids, lanes
        )
        for place, member in enumerate(joined):
            y_source_send[lanes, place : place + 1, :] = member[:, 0:1, :]
    to_y_peers(y_source_send, y_source_recv, source_send_sem, source_recv_sem)
    for lanes in groups:
        spread_coefs(y_coefs, lanes, row_y)
        spread_mids(y_mids, lanes, row_y)
    await_bytes(all_peers(y_matrix_recv, y_matrix_send), matrix_recv_sem)
    rings = []
    for lanes in groups:
        blocks = [
            tuple(
                y_matrix_recv[lanes, pl.ds(SUB * way + place, SUB, stride=SLOT_RUN), :]
                for place in range(3)
            )
            for way in range(WAYS)
        ]
        rings.append(tree_matrix(blocks, ring_coefs, lanes))

    await_bytes(all_peers(y_source_recv, y_source_send), source_recv_sem)

    for group, lanes in enumerate(groups):
        blocks = [
            tuple(
                y_source_recv[lanes, pl.ds(SUB * way + place, SUB, stride=SLOT_RUN), :]
                for place in range(2)
            )
            for way in range(WAYS)
        ]
        ring_source = tree_source(blocks, ring_coefs, ring_mids, lanes)
        own_value, prev_value = solve_pair(
            tuple(y_matrix_send[lanes, place : place + 1, :] for place in range(3)),
            tuple(y_source_send[lanes, place : place + 1, :] for place in range(2)),
            tuple(member[:, 0:1, :] for member in rings[group]),
            tuple(member[:, 0:1, :] for member in ring_source),
        )
        nodes = tree_down(
            jnp.broadcast_to(prev_value, shape_y),
            jnp.broadcast_to(own_value, shape_y),
            y_coefs,
            y_mids,
            lanes,
            row_y,
        )
        values = list(nodes[1:])
        for way in range(WAYS):
            out_ref[lanes, rows_of(way, length_y - 1, length_y), :] = values[way]
        for step in range(length_y - 2, -1, -1):
            for way in range(WAYS):
                values[way] = (
                    y_mid[step, way, lanes] + y_link[step, way, lanes] * nodes[way]
                ) + y_next[step, way, lanes] * values[way]
                out_ref[lanes, rows_of(way, step, length_y), :] = values[way]

    await_bytes(x_recv, x_send_sem)
    await_bytes(x_pair_recv, pair_send_sem)
    await_bytes(all_peers(y_matrix_recv, y_matrix_send), matrix_send_sem)
    await_bytes(all_peers(y_source_recv, y_source_send), source_send_sem)


def await_bytes(ref, sem):
    pltpu.make_async_copy(ref, ref, sem).wait()


def put_out(blocks_ref, out_hbm, sem):
    run = out_hbm.shape[0] // SUB
    stores = [
        pltpu.make_async_copy(
            blocks_ref.at[block, pl.ds((run + 1) * part, run)],
            out_hbm.at[pl.ds(run * part, run), pl.ds(LANES * block, LANES)],
            sem,
        )
        for block in range(blocks_ref.shape[0])
        for part in range(SUB)
    ]
    for store in stores:
        store.start()
    await_bytes(out_hbm, sem)


def body(initial_temp, kx_low, ky_low):
    count_x = lax.axis_size("gx")
    count_y = lax.axis_size("gy")
    _, rows, columns = initial_temp.shape
    length_x = columns // (WAYS * SUB)
    length_y = rows // (WAYS * SUB)
    blocks_x = rows // LANES
    blocks_y = columns // LANES

    def vmem(*shape):
        return pltpu.VMEM(shape, jnp.float32)

    def sems(*shape):
        return pltpu.SemaphoreType.DMA(shape)

    blocks = pl.pallas_call(
        functools.partial(kernel, count_x, count_y),
        out_shape=jax.ShapeDtypeStruct((blocks_y, rows + SUB, LANES), jnp.float32),
        in_specs=[pl.BlockSpec(memory_space=pltpu.HBM)] * 3,
        out_specs=pl.BlockSpec(memory_space=pltpu.VMEM),
        scratch_shapes=[
            vmem(rows, columns),
            vmem(rows, columns),
            vmem(rows, columns),
            vmem(blocks_y, rows + SUB, LANES),
            vmem(blocks_x, columns + SUB, LANES),
            vmem(blocks_x, columns + SUB, LANES),
            vmem(blocks_x, columns + SUB, LANES),
            vmem(blocks_y, rows + SUB, LANES),
            vmem(blocks_y, rows + SUB, LANES),
            vmem(blocks_y, rows + SUB, LANES),
            vmem(rows + SUB, LANES),
            vmem(rows + SUB, LANES),
            vmem(length_x - 1, WAYS, blocks_x, SUB, LANES),
            vmem(length_x - 1, WAYS, blocks_x, SUB, LANES),
            vmem(length_x - 1, WAYS, blocks_x, SUB, LANES),
            vmem(length_y - 1, WAYS, blocks_y, SUB, LANES),
            vmem(length_y - 1, WAYS, blocks_y, SUB, LANES),
            vmem(length_y - 1, WAYS, blocks_y, SUB, LANES),
            vmem(length_y - 1, WAYS, blocks_y, SUB, LANES),
            vmem(18, blocks_x, SUB, LANES),
            vmem(6, blocks_x, SUB, LANES),
            vmem(18, blocks_y, SUB, LANES),
            vmem(6, blocks_y, SUB, LANES),
            vmem(18, blocks_y, SUB, LANES),
            vmem(6, blocks_y, SUB, LANES),
            vmem(blocks_x, SUB, LANES),
            vmem(2, blocks_x, SUB, LANES),
            vmem(2 * REACH, blocks_x, SUB, LANES),
            vmem(2, blocks_x, SUB, LANES),
            vmem(blocks_y, 3, LANES),
            vmem(blocks_y, SUB * SLOT_RUN, LANES),
            vmem(blocks_y, 2, LANES),
            vmem(blocks_y, SUB * SLOT_RUN, LANES),
            sems(3),
        ]
        + [pltpu.SemaphoreType.DMA, sems(2)]
        + [pltpu.SemaphoreType.DMA] * 6
        + [pltpu.SemaphoreType.REGULAR] * 2,
        compiler_params=pltpu.CompilerParams(
            collective_id=0, has_side_effects=True, vmem_limit_bytes=ROOM
        ),
    )(*(pltpu.with_memory_space_constraint(value[0], pltpu.HBM) for value in (initial_temp, kx_low, ky_low)))
    result = pl.pallas_call(
        put_out,
        out_shape=jax.ShapeDtypeStruct((rows, columns), jnp.float32),
        in_specs=[pl.BlockSpec(memory_space=pltpu.VMEM)],
        out_specs=pl.BlockSpec(memory_space=pltpu.HBM),
        scratch_shapes=[pltpu.SemaphoreType.DMA],
        compiler_params=pltpu.CompilerParams(vmem_limit_bytes=SMALL_ROOM),
    )(blocks)
    return result[None]


def solution(mesh):
    spec = P(None, "gy", "gx")
    return jax.shard_map(
        body, mesh=mesh, in_specs=(spec, spec, spec), out_specs=spec, check_vma=False
    )
```
